32 devices in a mesh: row: 8 (over z, y), col: 4 (over x, core).
Axes of the slice: x: 2, y: 2, z: 4, core: 2. Of those that a mesh axis runs over, the one named last changes fastest.
Arguments:
- factor_band: float32 [1024, 131072], P('row', 'col'), may hold values from -0.015625 to 0.015625
- normals: float32 [131072, 96], P('col', 'row'), may hold values from -6 to 6
- site_mean: float32 [1024], P('row'), may hold values from 5 to 10
- site_spread: float32 [1024], P('row'), may hold values from 1 to 4
- site_capacity: float32 [1024], P('row'), may hold values from 0.1 to 1
- site_kind: int32 [1024], P('row'), may hold values 0 or 1
- site_plant: int32 [1024], P('row'), may hold values from 0 to 2047
Outputs:
- plant_output: float32 [96, 2048], P('col', 'row')
The draws below stay inside these ranges and needn't reach their ends.
All inputs are finite; a program needn't handle non-finite values. No bound on the sum of `site_kind` on one device may be relied on, other than what follows from the above.
Results may differ from the reference program's by a relative error of at most 0.000096.
Values sent between devices are 32-bit elements; how exact they have to be, the bound alone decides.
No kernel may reach another device: no remote copies, remote signals or barrier semaphores. Data moves between devices by JAX's collectives and lax.ppermute only.
A program may use at most 128 MiB of HBM per device.

```python
import math
import jax
import jax.numpy as jnp
import numpy as np
from jax import lax

N = 131072
PLANTS = 2048
BAND = 1024
SAMPLES = 96


def plant(drawn, key, low, high):
    index_at = [jax.random.randint(jax.random.fold_in(key, axis), (), 0, length) for axis, length in enumerate(drawn.shape)]
    main_axis = drawn.shape.index(max(drawn.shape))
    neighbour = index_at[:main_axis] + [(index_at[main_axis] + 1) % drawn.shape[main_axis]] + index_at[main_axis + 1:]
    return drawn.at[tuple(index_at)].set(low).at[tuple(neighbour)].set(high)


def block_levels(rng, dims, pieces, low, largest):
    def one(dim, blocks):
        steps = jax.random.uniform(jax.random.fold_in(jax.random.fold_in(rng, 6), dim), (blocks,), jnp.float32, low / len(pieces), largest / len(pieces))
        return jnp.repeat(jnp.exp(steps), dims[dim] // blocks).reshape((-1,) + (1,) * (len(dims) - dim - 1))

    loudness = one(*pieces[0])
    for cut in pieces[1:]:
        loudness = loudness * one(*cut)
    return loudness


def rank_bounds(number_of, skew):
    portions = [(1 << 20) // math.isqrt(standing ** skew) + 1 for standing in range(1, number_of + 1)]
    scale = 1 + sum(portions) // (1 << 30)
    return np.cumsum(np.array([max(1, weight // scale) for weight in portions]))


def ranked(own_key, dims, count, slope):
    listing = rank_bounds(count, slope)
    pick = jax.random.randint(jax.random.fold_in(own_key, 1), dims, 0, int(listing[count - 1]))
    grade = jnp.searchsorted(jnp.asarray(listing, jnp.int32), pick, side="right")
    return jax.random.permutation(jax.random.fold_in(own_key, 2), count)[grade].astype(jnp.int32)


def bell_draw(key, shape, width, most, pieces=(), kind=jnp.bfloat16):
    result = width * jax.random.normal(key, shape, jnp.float32)
    if pieces:
        result = result * block_levels(key, shape, pieces, -0.22, 0.18)
    return jnp.clip(result, -most, most).astype(kind)


def setup_inputs(seed: int = 0) -> dict:
    arg_keys = jax.random.split(jax.random.key(seed), 8)
    return {
        "factor_band": bell_draw(arg_keys[0], (BAND, N), N ** -0.5, 0.015625, ((0, 8), (1, 4)), jnp.float32),
        "normals": bell_draw(arg_keys[1], (N, SAMPLES), 1.0, 6.0, ((0, 4), (1, 8)), jnp.float32),
        "site_mean": jnp.clip(jnp.exp(math.log(10.0) - 0.6931472 * jax.random.uniform(arg_keys[2], (BAND,), jnp.float32) ** block_levels(arg_keys[2], (BAND,), ((0, 8),), -0.2, 0.2)), 5.0, 10.0),
        "site_spread": jnp.clip(jnp.exp(math.log(4.0) - 1.3862944 * jax.random.uniform(arg_keys[3], (BAND,), jnp.float32) ** block_levels(arg_keys[3], (BAND,), ((0, 8),), -0.2, 0.2)), 1.0, 4.0),
        "site_capacity": jnp.clip(jnp.exp(math.log(1.0) - 2.3025851 * jax.random.uniform(arg_keys[4], (BAND,), jnp.float32) ** block_levels(arg_keys[4], (BAND,), ((0, 8),), -0.2, 0.2)), 0.1, 1.0),
        "site_kind": plant((jax.random.randint(arg_keys[5], (BAND,), 0, 3) < 1).astype(jnp.int32), jax.random.fold_in(arg_keys[5], 1), 0, 1),
        "site_plant": plant(ranked(arg_keys[6], (BAND,), PLANTS, 1), jax.random.fold_in(arg_keys[6], 3), 0, PLANTS - 1).astype(jnp.int32),
    }


def reference(factor_band, normals, site_mean, site_spread, site_capacity, site_kind, site_plant):
    samples = lax.dot_general(normals, factor_band, (((0,), (1,)), ((), ())), precision=lax.Precision.HIGHEST, preferred_element_type=jnp.float32)
    speed = site_mean[None, :] + site_spread[None, :] * samples
    positive = jnp.maximum(speed, 0.0)
    wind = jnp.clip((positive * positive * positive - 27.0) / (1728.0 - 27.0), 0.0, 1.0)
    solar = jnp.clip(speed / 12.0, 0.0, 1.0)
    power = jnp.where(site_kind[None, :] == 1, solar, wind) * site_capacity[None, :]
    totals = jax.ops.segment_sum(power.T, site_plant, num_segments=PLANTS)
    return totals.T
```

```python
import math

import jax
import jax.numpy as jnp
from jax import lax
from jax.experimental import pallas as pl
from jax.experimental.pallas import tpu as pltpu
from jax.sharding import PartitionSpec as P

PLANTS = 2048
LANE = 128


def split_bf16(x):
    hi = x.astype(jnp.bfloat16)
    return hi, (x - hi.astype(jnp.float32)).astype(jnp.bfloat16)


def dot_t(a, b):
    return lax.dot_general(a, b, (((1,), (1,)), ((), ())), preferred_element_type=jnp.float32)


def step_width(width):
    tiles = width // LANE
    best = max(d for d in range(1, 17) if tiles % d == 0)
    return best * LANE


def products(blocks, factor, offset, folds, rows):
    width = blocks[0].shape[1]
    band, cols = factor.shape
    stride = cols // folds
    tk = step_width(width)
    total = sum(b.shape[0] for b in blocks)
    groups = total // (folds * rows)
    steps = width // tk

    def kernel(*refs):
        block_refs, factor_refs = refs[: len(blocks)], refs[len(blocks) : len(blocks) + folds]
        out_ref, acc = refs[-2], refs[-1]
        step = pl.program_id(0)

        @pl.when(step == 0)
        def _():
            acc[...] = jnp.zeros_like(acc)

        hi, lo = split_bf16(jnp.concatenate([r[...] for r in block_refs], axis=0))
        for fold in range(folds):
            f_hi, f_lo = split_bf16(factor_refs[fold][...])
            acc[fold] += dot_t(hi, f_hi) + (dot_t(hi, f_lo) + dot_t(lo, f_hi))

        @pl.when(step == steps - 1)
        def _():
            for g in range(groups):
                base = g * folds * rows
                out_ref[g] = sum(acc[fold, base + fold * rows : base + (fold + 1) * rows] for fold in range(folds))

    def factor_spec(fold):
        start = fold * stride + offset
        return pl.BlockSpec((pl.Element(band), pl.Element(tk)), lambda i: (0, pl.multiple_of(start + i * tk, LANE)))

    return pl.pallas_call(
        kernel,
        grid=(steps,),
        in_specs=[pl.BlockSpec((b.shape[0], tk), lambda i: (0, i)) for b in blocks]
        + [factor_spec(fold) for fold in range(folds)],
        out_specs=pl.BlockSpec((groups, rows, band), lambda i: (0, 0, 0)),
        out_shape=jax.ShapeDtypeStruct((groups, rows, band), jnp.float32),
        scratch_shapes=[pltpu.VMEM((folds, total, band), jnp.float32)],
    )(*blocks, *([factor] * folds))


def body(factor_band, normals, site_mean, site_spread, site_capacity, site_kind, site_plant):
    row_size, col_size = lax.axis_size("row"), lax.axis_size("col")
    row, col = lax.axis_index("row"), lax.axis_index("col")
    planes = row_size // 2
    z, y = row // 2, row % 2
    cols, rows = normals.shape
    band = factor_band.shape[0]
    folds = 8 // math.gcd(rows, 8)
    stride = cols // folds

    side = [(r, r ^ 1) for r in range(row_size)]

    def line(neighbour):
        return [(r, 2 * neighbour(r // 2) + r % 2) for r in range(row_size)]

    even = line(lambda p: p ^ 1)
    odd = line(lambda p: p if p in (0, planes - 1) else ((p - 1) ^ 1) + 1)
    send = lambda x, pairs: lax.ppermute(x, "row", pairs)
    heading = 1 - 2 * (z % 2)
    reach = jnp.where(heading == 1, planes - 1 - z, z)

    turned = normals.T
    tiles = stride // LANE
    first = max(1, round(tiles * 20 / 128))
    first += (tiles - first) % 2
    half = (tiles - first) // 2

    def piece(start, width):
        return jnp.concatenate(
            [turned[:, f * stride + start : f * stride + start + width] for f in range(folds)], axis=0
        )

    def along(own):
        from_even, from_odd = [own], [own]
        for j in range(1, planes):
            e = send(from_odd[j - 1], even)
            if j < planes - 1:
                from_odd.append(send(from_even[j - 1], odd))
            from_even.append(e)
        out = [from_even[1]]
        for j in range(2, planes):
            out.append(jnp.where(j <= reach, from_even[j], from_odd[planes - j]))
        return out

    parts = [[[], []] for _ in range(planes)]

    def multiply(items, start):
        got = products([b for b, _ in items], factor_band, start, folds, rows)
        g = 0
        for _, places in items:
            for j, q in places:
                parts[j][q].append(got[g])
                g += 1

    both = piece(0, first * LANE)
    both = jnp.concatenate([both, send(both, side)], axis=0)
    own_pieces = []
    for start in (first * LANE, (first + half) * LANE):
        own = piece(start, half * LANE)
        own_pieces.append((start, own, send(own, side), along(own)))
    both_others = along(both)
    multiply([(both, [(0, 0), (0, 1)]), (both_others[0], [(1, 0), (1, 1)])], 0)
    for start, own, beside, others in own_pieces:
        sides = [send(b, side) for b in others]
        multiply([(own, [(0, 0)]), (beside, [(0, 1)]), (others[0], [(1, 0)])], start)
        for j in range(1, planes - 1):
            multiply([(sides[j - 1], [(j, 1)]), (others[j], [(j + 1, 0)])], start)
        multiply([(sides[-1], [(planes - 1, 1)])], start)
    for j in range(1, planes - 1):
        multiply([(both_others[j], [(j + 1, 0), (j + 1, 1)])], 0)

    sums = [[sum(terms) for terms in pair] for pair in parts]
    share = rows * row_size // col_size
    placed = []
    for plane in range(planes):
        slot = jnp.mod(heading * (plane - z), planes)
        mine, other = sums[0]
        for j in range(1, planes):
            mine = jnp.where(slot == j, sums[j][0], mine)
            other = jnp.where(slot == j, sums[j][1], other)
        placed += [jnp.where(y == 0, mine, other), jnp.where(y == 0, other, mine)]
    total = jnp.concatenate(placed, axis=0).reshape(col_size, share, band)

    samples = lax.dynamic_index_in_dim(total, col, 0, keepdims=False)
    for k in range(1, col_size):
        pairs = [(c, c ^ k) for c in range(col_size)]
        samples = samples + lax.ppermute(lax.dynamic_index_in_dim(total, col ^ k, 0, keepdims=False), "col", pairs)

    speed = site_mean[None, :] + site_spread[None, :] * samples
    positive = jnp.maximum(speed, 0.0)
    wind = jnp.clip((positive * positive * positive - 27.0) / (1728.0 - 27.0), 0.0, 1.0)
    solar = jnp.clip(speed / 12.0, 0.0, 1.0)
    power = jnp.where(site_kind[None, :] == 1, solar, wind) * site_capacity[None, :]

    def spread(x, stack):
        pair = stack([x, send(x, side)])
        return [pair] + [
            send(pair, line(lambda p, k=k: p ^ k)) for k in range(1, planes)
        ]

    all_power = jnp.concatenate(spread(power, lambda v: jnp.concatenate(v, axis=1)), axis=1)
    plant = site_plant.astype(jnp.int32)
    all_plant = jnp.concatenate(spread(plant, lambda v: jnp.concatenate(v, axis=0)), axis=0)
    mine = PLANTS // row_size
    onehot = (
        all_plant[:, None] == row * mine + jnp.arange(mine, dtype=jnp.int32)[None, :]
    ).astype(jnp.float32)
    return jnp.dot(all_power, onehot, precision=lax.Precision.HIGHEST, preferred_element_type=jnp.float32)


def solution(mesh):
    in_specs = (P("row", "col"), P("col", "row"), P("row"), P("row"), P("row"), P("row"), P("row"))
    out_specs = P("col", "row")
    return jax.shard_map(body, mesh=mesh, in_specs=in_specs, out_specs=out_specs, check_vma=False)
```

```python
import math

import jax
import jax.numpy as jnp
from jax import lax
from jax.experimental import pallas as pl
from jax.experimental.pallas import tpu as pltpu
from jax.sharding import PartitionSpec as P


PLANTS = 2048
LANE = 128


def split_bf16(x):
    hi = x.astype(jnp.bfloat16)
    return hi, (x - hi.astype(jnp.float32)).astype(jnp.bfloat16)


def dot_t(a, b):
    return lax.dot_general(a, b, (((1,), (1,)), ((), ())), preferred_element_type=jnp.float32)


def step_width(width):
    tiles = width // LANE
    return LANE * max(d for d in range(1, 29) if tiles % d == 0 and (d < tiles or tiles == 1))


def products(blocks, factor, offset, folds, rows):
    width = blocks[0].shape[1]
    band, cols = factor.shape
    stride = cols // folds
    tk = step_width(width)
    total = sum(b.shape[0] for b in blocks)
    groups = total // (folds * rows)
    steps = width // tk

    def kernel(*refs):
        block_refs, factor_refs = refs[: len(blocks)], refs[len(blocks) : len(blocks) + folds]
        out_ref, acc = refs[-2], refs[-1]
        step = pl.program_id(0)

        @pl.when(step == 0)
        def _():
            acc[...] = jnp.zeros_like(acc)

        hi, lo = split_bf16(jnp.concatenate([r[...] for r in block_refs], axis=0))
        both = jnp.concatenate([hi, lo], axis=0)
        for fold in range(folds):
            f_hi, f_lo = split_bf16(factor_refs[fold][...])
            first = dot_t(both, f_hi)
            acc[fold] += first[:total] + (first[total:] + dot_t(hi, f_lo))

        @pl.when(step == steps - 1)
        def _():
            for g in range(groups):
                base = g * folds * rows
                out_ref[g] = sum(acc[fold, base + fold * rows : base + (fold + 1) * rows] for fold in range(folds))

    def factor_spec(fold):
        start = fold * stride + offset
        return pl.BlockSpec((pl.Element(band), pl.Element(tk)), lambda i: (0, pl.multiple_of(start + i * tk, LANE)))

    return pl.pallas_call(
        kernel,
        grid=(steps,),
        in_specs=[pl.BlockSpec((b.shape[0], tk), lambda i: (0, i)) for b in blocks]
        + [factor_spec(fold) for fold in range(folds)],
        out_specs=pl.BlockSpec((groups, rows, band), lambda i: (0, 0, 0)),
        out_shape=jax.ShapeDtypeStruct((groups, rows, band), jnp.float32),
        scratch_shapes=[pltpu.VMEM((folds, total, band), jnp.float32)],
    )(*blocks, *([factor] * folds))


CHUNKS = 2


def arriving(t, planes):
    if t == 1:
        return [1]
    return sorted({t, planes - t} - {1}) if 2 * t >= planes else []


def plan(planes):
    chunks = [str(c) for c in range(CHUNKS)]
    last = planes - 1
    steps = [("b", "y", 0)]
    for c in chunks:
        steps += [(c, "e", 1), (c, "y", 0)] + [(c, "m", 1)] * (last > 1)
    steps += [("b", "e", 1)] + [("b", "m", 1)] * (last > 1)
    steps += [(c, "mul", (("slot", 0),)) for c in chunks]
    sent = [0]
    for t in range(1, planes):
        new = arriving(t, planes)
        if t == last:
            for j in range(2, planes):
                steps += [("b", "e", j)] + [("b", "m", j + 1)] * (j + 1 < last)
        for c in chunks:
            steps += [(c, "y", j) for j in new]
            if t < last:
                steps += [(c, "m", t + 1)] * (t + 1 < last) + [(c, "e", t + 1)]
            if t == 1 and c == chunks[0] and last > 2:
                steps += [("b", "m", 2)]
            if sent or new:
                steps += [(c, "mul", tuple([("y", j) for j in sent] + [("slot", j) for j in new]))]
        if t == 1:
            steps += [("b", "mul", (("slot", 0), ("slot", 1)))]
        sent = new
    for t in range(2, last):
        if arriving(t, planes):
            steps += [("b", "mul", tuple(("slot", j) for j in arriving(t, planes)))]
    steps += [(c, "mul", tuple(("y", j) for j in sent)) for c in chunks[:-1]]
    if last > 1:
        steps += [("b", "mul", (("slot", last),))]
    steps += [(c, "mul", tuple(("y", j) for j in sent)) for c in chunks[-1:]]
    return steps


def body(factor_band, normals, site_mean, site_spread, site_capacity, site_kind, site_plant):
    row_size, col_size = lax.axis_size("row"), lax.axis_size("col")
    row, col = lax.axis_index("row"), lax.axis_index("col")
    planes = row_size // 2
    z, y = row // 2, row % 2
    cols, rows = normals.shape
    band = factor_band.shape[0]
    folds = 8 // math.gcd(rows, 8)
    stride = cols // folds

    side = [(r, r ^ 1) for r in range(row_size)]

    def line(neighbour):
        return [(r, 2 * neighbour(r // 2) + r % 2) for r in range(row_size)]

    even = line(lambda p: p ^ 1)
    odd = line(lambda p: p if p in (0, planes - 1) else ((p - 1) ^ 1) + 1)
    send = lambda x, pairs: lax.ppermute(x, "row", pairs)
    heading = 1 - 2 * (z % 2)
    reach = jnp.where(heading == 1, planes - 1 - z, z)

    turned = normals.T
    tiles = stride // LANE
    first = max(1, round(tiles * 20 / 128))
    first += (tiles - first) % CHUNKS
    part = (tiles - first) // CHUNKS

    def piece(start, width):
        return jnp.concatenate(
            [turned[:, f * stride + start : f * stride + start + width] for f in range(folds)], axis=0
        )

    have, begin = {}, {"b": 0}
    small = piece(0, first * LANE)
    for c in range(CHUNKS):
        begin[str(c)] = (first + c * part) * LANE
        have[str(c), "slot", 0] = piece(begin[str(c)], part * LANE)

    def slot(stream, j):
        key = stream, "slot", j
        if key not in have:
            e = have[stream, "e", j]
            have[key] = e if j == 1 else jnp.where(j <= reach, e, have[stream, "m", planes - j])
        return have[key]

    parts = [[[], []] for _ in range(planes)]

    def multiply(stream, wanted):
        blocks, places = [], []
        for kind, j in wanted:
            blocks.append(slot(stream, j) if kind == "slot" else have[stream, kind, j])
            places += [(j, 0), (j, 1)] if stream == "b" else [(j, int(kind == "y"))]
        got = products(blocks, factor_band, begin[stream], folds, rows)
        for g, (j, q) in enumerate(places):
            parts[j][q].append(got[g])

    for step in plan(planes):
        stream, move, j = step
        if move == "mul":
            multiply(stream, j)
        elif step == ("b", "y", 0):
            have["b", "slot", 0] = jnp.concatenate([small, send(small, side)], axis=0)
        elif move == "y":
            have[stream, "y", j] = send(slot(stream, j), side)
        else:
            came = have[stream, "m" if move == "e" else "e", j - 1] if j > 1 else slot(stream, 0)
            have[step] = send(came, even if move == "e" else odd)

    sums = [[sum(terms) for terms in pair] for pair in parts]
    share = rows * row_size // col_size
    placed = []
    for plane in range(planes):
        at = jnp.mod(heading * (plane - z), planes)
        mine, other = sums[0]
        for j in range(1, planes):
            mine = jnp.where(at == j, sums[j][0], mine)
            other = jnp.where(at == j, sums[j][1], other)
        placed += [jnp.where(y == 0, mine, other), jnp.where(y == 0, other, mine)]
    total = jnp.concatenate(placed, axis=0).reshape(col_size, share, band)

    samples = lax.dynamic_index_in_dim(total, col, 0, keepdims=False)
    for k in range(1, col_size):
        pairs = [(c, c ^ k) for c in range(col_size)]
        samples = samples + lax.ppermute(lax.dynamic_index_in_dim(total, col ^ k, 0, keepdims=False), "col", pairs)

    speed = site_mean[None, :] + site_spread[None, :] * samples
    positive = jnp.maximum(speed, 0.0)
    wind = jnp.clip((positive * positive * positive - 27.0) / (1728.0 - 27.0), 0.0, 1.0)
    solar = jnp.clip(speed / 12.0, 0.0, 1.0)
    power = jnp.where(site_kind[None, :] == 1, solar, wind) * site_capacity[None, :]

    power = jnp.concatenate([power, site_plant[None, :].astype(jnp.float32)], axis=0)
    pair = jnp.concatenate([power, send(power, side)], axis=1)
    table = jnp.concatenate(
        [pair] + [send(pair, line(lambda p, k=k: p ^ k)) for k in range(1, planes)], axis=1
    )
    plant = table[share].astype(jnp.int32)
    mine = PLANTS // row_size
    onehot = (plant[:, None] == row * mine + jnp.arange(mine, dtype=jnp.int32)[None, :]).astype(jnp.float32)
    return jnp.dot(table[:share], onehot, precision=lax.Precision.HIGHEST, preferred_element_type=jnp.float32)


def solution(mesh):
    in_specs = (P("row", "col"), P("col", "row"), P("row"), P("row"), P("row"), P("row"), P("row"))
    out_specs = P("col", "row")
    return jax.shard_map(body, mesh=mesh, in_specs=in_specs, out_specs=out_specs, check_vma=False)
```

```python
import math

import jax
import jax.numpy as jnp
from jax import lax
from jax.experimental import pallas as pl
from jax.experimental.pallas import tpu as pltpu
from jax.sharding import PartitionSpec as P


PLANTS = 2048
LANE = 128


def split_bf16(x):
    hi = x.astype(jnp.bfloat16)
    return hi, (x - hi.astype(jnp.float32)).astype(jnp.bfloat16)


def dot_t(a, b):
    return lax.dot_general(a, b, (((1,), (1,)), ((), ())), preferred_element_type=jnp.float32)


def step_width(width):
    tiles = width // LANE
    return LANE * max(d for d in range(1, 29) if tiles % d == 0 and (d < tiles or tiles == 1))


def products(blocks, factors, starts, rows):
    folds = len(factors)
    width = blocks[0].shape[1]
    band = factors[0].shape[0]
    tk = step_width(width)
    total = sum(b.shape[0] for b in blocks)
    groups = total // (folds * rows)
    steps = width // tk

    def kernel(*refs):
        block_refs, factor_refs = refs[: len(blocks)], refs[len(blocks) : len(blocks) + folds]
        out_ref, acc = refs[-2], refs[-1]
        step = pl.program_id(0)

        @pl.when(step == 0)
        def _():
            acc[...] = jnp.zeros_like(acc)

        hi, lo = split_bf16(jnp.concatenate([r[...] for r in block_refs], axis=0))
        both = jnp.concatenate([hi, lo], axis=0)
        for fold in range(folds):
            f_hi, f_lo = split_bf16(factor_refs[fold][...])
            first = dot_t(both, f_hi)
            acc[fold] += first[:total] + (first[total:] + dot_t(hi, f_lo))

        @pl.when(step == steps - 1)
        def _():
            for g in range(groups):
                base = g * folds * rows
                out_ref[g] = sum(acc[fold, base + fold * rows : base + (fold + 1) * rows] for fold in range(folds))

    def factor_spec(fold):
        start = starts[fold]
        return pl.BlockSpec((pl.Element(band), pl.Element(tk)), lambda i: (0, pl.multiple_of(start + i * tk, LANE)))

    return pl.pallas_call(
        kernel,
        grid=(steps,),
        in_specs=[pl.BlockSpec((b.shape[0], tk), lambda i: (0, i)) for b in blocks]
        + [factor_spec(fold) for fold in range(folds)],
        out_specs=pl.BlockSpec((groups, rows, band), lambda i: (0, 0, 0)),
        out_shape=jax.ShapeDtypeStruct((groups, rows, band), jnp.float32),
        scratch_shapes=[pltpu.VMEM((folds, total, band), jnp.float32)],
    )(*blocks, *factors)


CHUNKS = 2


def choose(flag, a, b):
    def kernel(flag_ref, a_ref, b_ref, out_ref, sem):
        @pl.when(flag_ref[0] == 1)
        def _():
            copy = pltpu.make_async_copy(a_ref, out_ref, sem)
            copy.start()
            copy.wait()

        @pl.when(flag_ref[0] != 1)
        def _():
            copy = pltpu.make_async_copy(b_ref, out_ref, sem)
            copy.start()
            copy.wait()

    anywhere = pl.BlockSpec(memory_space=pl.ANY)
    return pl.pallas_call(
        kernel,
        in_specs=[pl.BlockSpec(memory_space=pltpu.SMEM), anywhere, anywhere],
        out_specs=anywhere,
        out_shape=jax.ShapeDtypeStruct(a.shape, a.dtype),
        scratch_shapes=[pltpu.SemaphoreType.DMA],
    )(flag.astype(jnp.int32).reshape(1), a, b)


def arriving(t, planes):
    if t == 1:
        return [1]
    return sorted({t, planes - t} - {1}) if 2 * t >= planes else []


def exports(planes):
    return planes == 4


def plan(planes):
    slots = lambda *js: tuple(("slot", j) for j in js)
    if exports(planes):
        return (
            [("b", "y", 0), ("0", "e", 1), ("0", "m", 1), ("x", "y", 0), ("1", "e", 1), ("0", "y", 0), ("1", "m", 1)]
            + [("1", "y", 0), ("b", "e", 1), ("x", "e", 1), ("x", "f", 0), ("x", "f", 1)]
            + [("0", "mul", slots(0))]
            + [("0", "y", 1), ("0", "m", 2), ("0", "e", 2), ("1", "mul", slots(0))]
            + [("1", "y", 1), ("1", "m", 2), ("1", "e", 2), ("b", "m", 1), ("x", "m", 1)]
            + [("0", "mul", (("y", 0), ("slot", 1))), ("b", "m", 2), ("1", "mul", (("y", 0), ("slot", 1)))]
            + [("0", "sel", 2), ("0", "y", 2), ("0", "e", 3), ("x", "m", 2), ("b", "mul", slots(0, 1))]
            + [("1", "sel", 2), ("1", "y", 2), ("1", "e", 3), ("b", "e", 2)]
            + [("0", "mul", (("y", 1), ("slot", 2)))]
            + [("0", "sel", 3), ("0", "y", 3), ("1", "mul", (("y", 1), ("slot", 2)))]
            + [("1", "sel", 3), ("1", "y", 3), ("b", "e", 3)]
            + [("0", "mul", (("y", 2), ("slot", 3))), ("1", "mul", (("y", 2), ("slot", 3)))]
            + [("x", "mul", "own"), ("x", "mul", "far"), ("x", "back", 0)]
            + [("b", "sel", 2), ("b", "mul", slots(2)), ("0", "mul", (("y", 3),))]
            + [("b", "sel", 3), ("b", "mul", slots(3)), ("1", "mul", (("y", 3),))]
        )
    chunks = [str(c) for c in range(CHUNKS)]
    last = planes - 1
    steps = [("b", "y", 0)]
    for c in chunks:
        steps += [(c, "e", 1), (c, "y", 0)] + [(c, "m", 1)] * (last > 1)
    steps += [("b", "e", 1)] + [("b", "m", 1)] * (last > 1)
    steps += [(c, "mul", slots(0)) for c in chunks]
    sent = [0]
    for t in range(1, planes):
        new = arriving(t, planes)
        if t == last:
            for j in range(2, planes):
                steps += [("b", "e", j)] + [("b", "m", j + 1)] * (1 < j < last - 1)
        for c in chunks:
            for j in new:
                steps += [(c, "sel", j)] * (j > 1) + [(c, "y", j)]
            if t < last:
                steps += [(c, "m", t + 1)] * (t + 1 < last) + [(c, "e", t + 1)]
            if t == 1 and c == chunks[-1] and last > 2:
                steps += [("b", "m", 2)]
            if sent or new:
                steps += [(c, "mul", tuple(("y", j) for j in sent) + slots(*new))]
        if t == 1:
            steps += [("b", "mul", slots(0, 1))]
        sent = new
    for t in range(2, last):
        if arriving(t, planes):
            steps += [("b", "sel", j) for j in arriving(t, planes)] + [("b", "mul", slots(*arriving(t, planes)))]
    steps += [(c, "mul", tuple(("y", j) for j in sent)) for c in chunks[:-1]]
    if last > 1:
        steps += [("b", "sel", last), ("b", "mul", slots(last))]
    steps += [(c, "mul", tuple(("y", j) for j in sent)) for c in chunks[-1:]]
    return steps


def body(factor_band, normals, site_mean, site_spread, site_capacity, site_kind, site_plant):
    row_size, col_size = lax.axis_size("row"), lax.axis_size("col")
    row, col = lax.axis_index("row"), lax.axis_index("col")
    planes = row_size // 2
    z, y = row // 2, row % 2
    cols, rows = normals.shape
    band = factor_band.shape[0]
    folds = 8 // math.gcd(rows, 8)
    stride = cols // folds

    side = [(r, r ^ 1) for r in range(row_size)]

    def line(neighbour):
        return [(r, 2 * neighbour(r // 2) + r % 2) for r in range(row_size)]

    even = line(lambda p: p ^ 1)
    odd = line(lambda p: p if p in (0, planes - 1) else ((p - 1) ^ 1) + 1)
    send = lambda x, pairs: lax.ppermute(x, "row", pairs)
    heading = 1 - 2 * (z % 2)
    reach = jnp.where(heading == 1, planes - 1 - z, z)

    outer = (z == 0) | (z == planes - 1)

    def between(pairs, take):
        return [(a, b) for a, b in pairs if take(a // 2 in (0, planes - 1))]

    inward = between(even, lambda is_outer: is_outer)
    outward = between(even, lambda is_outer: not is_outer)

    turned = normals.T
    tiles = stride // LANE
    pairs_of = lambda share: 2 * round(tiles * share / 2)
    sizes = {"x": pairs_of(18 / 128), "b": pairs_of(22 / 128)} if exports(planes) else {"b": pairs_of(20 / 128)}
    rest = tiles - sum(sizes.values())
    sizes["1"] = 2 * (rest * 5 // 22)
    sizes["0"] = rest - sizes["1"]
    begin, at = {}, 0
    for stream in sizes:
        begin[stream], at = at * LANE, at + sizes[stream]

    def piece(stream):
        start, width = begin[stream], sizes[stream] * LANE
        return jnp.concatenate(
            [turned[:, f * stride + start : f * stride + start + width] for f in range(folds)], axis=0
        )

    own = {stream: piece(stream) for stream in ("b", "0", "x", "1") if stream in sizes}
    have = {(stream, "slot", 0): own[stream] for stream in ("0", "1")}
    parts = [[[], []] for _ in range(planes)]
    far = [[None, None] for _ in range(planes)]

    def starts_of(stream):
        return [f * stride + begin[stream] for f in range(folds)]

    def multiply(stream, wanted):
        blocks, places = [], []
        for kind, j in wanted:
            blocks.append(have[stream, kind, j])
            places += [(j, 0), (j, 1)] if stream == "b" else [(j, int(kind == "y"))]
        got = products(blocks, [factor_band] * folds, starts_of(stream), rows)
        for g, (j, q) in enumerate(places):
            parts[j][q].append(got[g])

    def multiply_exported(whose):
        blocks = [have["x", "slot", 0], have["x", "e", 1], have["x", "m", 1], have["x", "m", 2]]
        places = [(j % planes, q) for j in (0, 1, -1, -2) for q in (0, 1)]
        if whose == "own":
            got = products(blocks, [factor_band] * folds, starts_of("x"), rows)
            for g, (j, q) in enumerate(places):
                parts[j][q].append(jnp.where(outer, 0.0, got[g]))
        else:
            got = products(blocks, [have["x", "f", f] for f in range(folds)], [0] * folds, rows)
            for g, (j, q) in enumerate(places):
                far[j][q] = got[g]

    def place(sums):
        placed = []
        for plane in range(planes):
            at = jnp.mod(heading * (plane - z), planes)
            mine, other = sums[0]
            for j in range(1, planes):
                mine = jnp.where(at == j, sums[j][0], mine)
                other = jnp.where(at == j, sums[j][1], other)
            placed += [jnp.where(y == 0, mine, other), jnp.where(y == 0, other, mine)]
        return jnp.concatenate(placed, axis=0)

    for step in plan(planes):
        stream, move, j = step
        if move == "mul":
            multiply_exported(j) if stream == "x" else multiply(stream, j)
        elif move == "back":
            back = send(place(far), outward)
        elif move == "f":
            if j < folds:
                start = starts_of("x")[j]
                have[step] = send(factor_band[:, start : start + sizes["x"] * LANE], inward)
        elif move == "sel":
            have[stream, "slot", j] = choose(j <= reach, have[stream, "e", j], have[stream, "m", planes - j])
        elif move == "y" and stream in ("b", "x"):
            have[stream, "slot", 0] = jnp.concatenate([own[stream], send(own[stream], side)], axis=0)
        elif move == "y":
            have[step] = send(have[stream, "slot", j], side)
        else:
            came = have[stream, "m" if move == "e" else "e", j - 1] if j > 1 else have[stream, "slot", 0]
            pairs = odd if move == "m" else inward if stream == "x" else even
            if exports(planes) and move == "e" and j > 1:
                pairs = outward
            have[step] = send(came, pairs)
            if move == "e" and j == 1:
                have[stream, "slot", 1] = have[step]

    total = place([[sum(terms) for terms in pair] for pair in parts])
    if exports(planes):
        total = total + jnp.where(outer, back, 0.0)
    share = rows * row_size // col_size
    total = total.reshape(col_size, share, band)

    samples = lax.dynamic_index_in_dim(total, col, 0, keepdims=False)
    for k in range(1, col_size):
        pairs = [(c, c ^ k) for c in range(col_size)]
        samples = samples + lax.ppermute(lax.dynamic_index_in_dim(total, col ^ k, 0, keepdims=False), "col", pairs)

    speed = site_mean[None, :] + site_spread[None, :] * samples
    positive = jnp.maximum(speed, 0.0)
    wind = jnp.clip((positive * positive * positive - 27.0) / (1728.0 - 27.0), 0.0, 1.0)
    solar = jnp.clip(speed / 12.0, 0.0, 1.0)
    power = jnp.where(site_kind[None, :] == 1, solar, wind) * site_capacity[None, :]

    power = jnp.concatenate([power, site_plant[None, :].astype(jnp.float32)], axis=0)
    pair = jnp.concatenate([power, send(power, side)], axis=1)
    table = jnp.concatenate(
        [pair] + [send(pair, line(lambda p, k=k: p ^ k)) for k in range(1, planes)], axis=1
    )
    plant = table[share].astype(jnp.int32)
    mine = PLANTS // row_size
    onehot = (plant[:, None] == row * mine + jnp.arange(mine, dtype=jnp.int32)[None, :]).astype(jnp.float32)
    return jnp.dot(table[:share], onehot, precision=lax.Precision.HIGHEST, preferred_element_type=jnp.float32)


def solution(mesh):
    in_specs = (P("row", "col"), P("col", "row"), P("row"), P("row"), P("row"), P("row"), P("row"))
    out_specs = P("col", "row")
    return jax.shard_map(body, mesh=mesh, in_specs=in_specs, out_specs=out_specs, check_vma=False)
```

```python
import math

import jax
import jax.numpy as jnp
from jax import lax
from jax.experimental import pallas as pl
from jax.experimental.pallas import tpu as pltpu
from jax.sharding import PartitionSpec as P


PLANTS = 2048
LANE = 128


def split_bf16(x):
    hi = x.astype(jnp.bfloat16)
    return hi, (x - hi.astype(jnp.float32)).astype(jnp.bfloat16)


def dot_t(a, b):
    return lax.dot_general(a, b, (((1,), (1,)), ((), ())), preferred_element_type=jnp.float32)


def step_width(width):
    tiles = width // LANE
    return LANE * max(d for d in range(1, 29) if tiles % d == 0 and (d < tiles or tiles == 1))


def products(blocks, factors, starts, rows, band, order=None):
    folds = len(factors)
    arrays, specs, flags, places = [], [], [], []
    width = (blocks[0][1] if isinstance(blocks[0], tuple) else blocks[0]).shape[1]
    tk = step_width(width)
    steps = width // tk
    total = 0
    for block in blocks:
        if isinstance(block, tuple):
            flag, a, b = block
            k = len(flags)
            flags.append(flag)
            places.append((len(arrays), k))
            arrays += [a, b]
            specs.append(pl.BlockSpec((a.shape[0], tk), lambda i, s, k=k: (0, i * s[k])))
            specs.append(pl.BlockSpec((a.shape[0], tk), lambda i, s, k=k: (0, i * (1 - s[k]))))
        else:
            a = block
            places.append((len(arrays), None))
            arrays.append(a)
            specs.append(pl.BlockSpec((a.shape[0], tk), lambda i, s: (0, i)))
        total += a.shape[0]
    groups = total // (folds * rows)
    if order is None:
        order = range(groups)
    scalars = jnp.stack([jnp.asarray(s, jnp.int32) for s in flags + list(order)])

    for fold in range(folds):
        top, left = starts[fold]
        specs.append(
            pl.BlockSpec(
                (pl.Element(band), pl.Element(tk)),
                lambda i, s, top=top, left=left: (top, pl.multiple_of(left + i * tk, LANE)),
            )
        )

    def kernel(scalar_ref, *refs):
        out_ref, acc = refs[-2], refs[-1]
        factor_refs = refs[len(arrays) : len(arrays) + folds]
        step = pl.program_id(0)

        @pl.when(step == 0)
        def _():
            acc[...] = jnp.zeros_like(acc)

        taken = [
            refs[i][...] if k is None else jnp.where(scalar_ref[k] == 1, refs[i][...], refs[i + 1][...])
            for i, k in places
        ]
        hi, lo = split_bf16(jnp.concatenate(taken, axis=0))
        both = jnp.concatenate([hi, lo], axis=0)
        for fold in range(folds):
            f_hi, f_lo = split_bf16(factor_refs[fold][...])
            first = dot_t(both, f_hi)
            acc[fold] += first[:total] + (first[total:] + dot_t(hi, f_lo))

        @pl.when(step == steps - 1)
        def _():
            for g in range(groups):
                base = g * folds * rows
                out_ref[scalar_ref[len(flags) + g]] = sum(
                    acc[fold, base + fold * rows : base + (fold + 1) * rows] for fold in range(folds)
                )

    return pl.pallas_call(
        kernel,
        grid_spec=pltpu.PrefetchScalarGridSpec(
            num_scalar_prefetch=1,
            grid=(steps,),
            in_specs=specs,
            out_specs=pl.BlockSpec((groups, rows, band), lambda i, s: (0, 0, 0)),
            scratch_shapes=[pltpu.VMEM((folds, total, band), jnp.float32)],
        ),
        out_shape=jax.ShapeDtypeStruct((groups, rows, band), jnp.float32),
    )(scalars, *arrays, *factors)


CHUNKS = 2


def choose(flag, a, b):
    height, width = a.shape
    tk = step_width(width)

    def kernel(flag_ref, a_ref, b_ref, out_ref):
        @pl.when(flag_ref[0] == 1)
        def _():
            out_ref[...] = a_ref[...]

        @pl.when(flag_ref[0] != 1)
        def _():
            out_ref[...] = b_ref[...]

    return pl.pallas_call(
        kernel,
        grid_spec=pltpu.PrefetchScalarGridSpec(
            num_scalar_prefetch=1,
            grid=(width // tk,),
            in_specs=[
                pl.BlockSpec((height, tk), lambda i, flag: (0, i * flag[0])),
                pl.BlockSpec((height, tk), lambda i, flag: (0, i * (1 - flag[0]))),
            ],
            out_specs=pl.BlockSpec((height, tk), lambda i, flag: (0, i)),
        ),
        out_shape=jax.ShapeDtypeStruct(a.shape, a.dtype),
    )(flag.astype(jnp.int32).reshape(1), a, b)


def arriving(t, planes):
    if t == 1:
        return [1]
    return sorted({t, planes - t} - {1}) if 2 * t >= planes else []


def exports(planes):
    return planes == 4


def plan(planes):
    slots = lambda *js: tuple(("slot", j) for j in js)
    if exports(planes):
        near = slots(0) + (("y", 0),) + slots(1)
        inner = (("y", 1),) + slots(2) + (("y", 2),) + slots(3)
        return (
            [("bx", "y", 0), ("0", "e", 1), ("0", "m", 1), ("1", "e", 1), ("0", "y", 0), ("1", "m", 1), ("1", "y", 0)]
            + [("b", "e", 1), ("x", "e", 1), ("x", "f", 0)]
            + [("0", "y", 1), ("0", "m", 2), ("0", "e", 2), ("0", "mul", near)]
            + [("1", "y", 1), ("1", "m", 2), ("1", "e", 2), ("bx", "m", 1)]
            + [("b", "m", 2), ("1", "mul", near)]
            + [("0", "sel", 2), ("0", "y", 2), ("0", "e", 3), ("x", "m", 2)]
            + [("1", "sel", 2), ("1", "y", 2), ("1", "e", 3), ("b", "e", 2), ("b", "mul", slots(0, 1))]
            + [("0", "sel", 3), ("0", "y", 3)]
            + [("1", "sel", 3), ("1", "y", 3), ("b", "e", 3)]
            + [("x", "mul", "own"), ("0", "mul", inner), ("x", "mul", "far"), ("x", "back", 0)]
            + [("1", "mul", inner), ("0", "mul", (("y", 3),)), ("b", "mul", slots(2, 3)), ("1", "mul", (("y", 3),))]
        )
    chunks = [str(c) for c in range(CHUNKS)]
    last = planes - 1
    steps = [("bx", "y", 0)]
    for c in chunks:
        steps += [(c, "e", 1), (c, "y", 0)] + [(c, "m", 1)] * (last > 1)
    steps += [("b", "e", 1)] + [("b", "m", 1)] * (last > 1)
    steps += [(c, "mul", slots(0)) for c in chunks]
    sent = [0]
    for t in range(1, planes):
        new = arriving(t, planes)
        if t == last:
            for j in range(2, planes):
                steps += [("b", "e", j)] + [("b", "m", j + 1)] * (1 < j < last - 1)
        for c in chunks:
            for j in new:
                steps += [(c, "sel", j)] * (j > 1) + [(c, "y", j)]
            if t < last:
                steps += [(c, "m", t + 1)] * (t + 1 < last) + [(c, "e", t + 1)]
            if t == 1 and c == chunks[-1] and last > 2:
                steps += [("b", "m", 2)]
            if sent or new:
                steps += [(c, "mul", tuple(("y", j) for j in sent) + slots(*new))]
        if t == 1:
            steps += [("b", "mul", slots(0, 1))]
        sent = new
    for t in range(2, last):
        if arriving(t, planes):
            steps += [("b", "mul", slots(*arriving(t, planes)))]
    steps += [(c, "mul", tuple(("y", j) for j in sent)) for c in chunks[:-1]]
    if last > 1:
        steps += [("b", "mul", slots(last))]
    steps += [(c, "mul", tuple(("y", j) for j in sent)) for c in chunks[-1:]]
    return steps


def body(factor_band, normals, site_mean, site_spread, site_capacity, site_kind, site_plant):
    row_size, col_size = lax.axis_size("row"), lax.axis_size("col")
    row, col = lax.axis_index("row"), lax.axis_index("col")
    planes = row_size // 2
    z, y = row // 2, row % 2
    cols, rows = normals.shape
    band = factor_band.shape[0]
    folds = 8 // math.gcd(rows, 8)
    stride = cols // folds

    side = [(r, r ^ 1) for r in range(row_size)]

    def line(neighbour):
        return [(r, 2 * neighbour(r // 2) + r % 2) for r in range(row_size)]

    even = line(lambda p: p ^ 1)
    odd = line(lambda p: p if p in (0, planes - 1) else ((p - 1) ^ 1) + 1)
    send = lambda x, pairs: lax.ppermute(x, "row", pairs)
    heading = 1 - 2 * (z % 2)
    reach = jnp.where(heading == 1, planes - 1 - z, z)

    outer = (z == 0) | (z == planes - 1)

    def between(pairs, take):
        return [(a, b) for a, b in pairs if take(a // 2 in (0, planes - 1))]

    inward = between(even, lambda is_outer: is_outer)
    outward = between(even, lambda is_outer: not is_outer)

    turned = normals.T
    tiles = stride // LANE
    pairs_of = lambda share: 2 * round(tiles * share / 2)
    sizes = {"x": pairs_of(18 / 128), "b": pairs_of(22 / 128)} if exports(planes) else {"b": pairs_of(20 / 128)}
    rest = tiles - sum(sizes.values())
    sizes["1"] = 2 * (rest * 5 // 22)
    sizes["0"] = rest - sizes["1"]
    begin, at = {}, 0
    for stream in sizes:
        begin[stream], at = at * LANE, at + sizes[stream]

    begin["bx"], sizes["bx"] = 0, sizes["b"] + sizes.get("x", 0)

    def piece(stream):
        start, width = begin[stream], sizes[stream] * LANE
        return jnp.concatenate(
            [turned[:, f * stride + start : f * stride + start + width] for f in range(folds)], axis=0
        )

    own = {stream: piece(stream) for stream in ("bx", "0", "1")}
    have = {(stream, "slot", 0): own[stream] for stream in ("0", "1")}
    parts = [[[], []] for _ in range(planes)]

    def starts_of(stream):
        return [(0, f * stride + begin[stream]) for f in range(folds)]

    def cut(stream, block):
        return block[:, begin[stream] : begin[stream] + sizes[stream] * LANE]

    def multiply(stream, wanted):
        blocks, places = [], []
        for kind, j in wanted:
            if stream == "b" and j > 1:
                blocks.append((j <= reach, have["b", "e", j], have["b", "m", planes - j]))
            else:
                blocks.append(have[stream, kind, j])
            places += [(j, 0), (j, 1)] if stream == "b" else [(j, int(kind == "y"))]
        got = products(blocks, [factor_band] * folds, starts_of(stream), rows, band)
        for g, (j, q) in enumerate(places):
            parts[j][q].append(got[g])

    def multiply_exported(whose):
        blocks = [have["x", "slot", 0], have["x", "e", 1], have["x", "m", 1], have["x", "m", 2]]
        places = [(j % planes, q) for j in (0, 1, -1, -2) for q in (0, 1)]
        if whose == "own":
            got = products(blocks, [factor_band] * folds, starts_of("x"), rows, band)
            for g, (j, q) in enumerate(places):
                parts[j][q].append(jnp.where(outer, 0.0, got[g]))
        else:
            order = [
                2 * jnp.mod(z + heading * j, planes) + (y if q == 0 else 1 - y) for j, q in places
            ]
            have["x", "far", 0] = products(
                blocks, [have["x", "f", 0]] * folds, [(f * band, 0) for f in range(folds)], rows, band, order
            ).reshape(row_size * rows, band)

    def place(sums):
        placed = []
        for plane in range(planes):
            at = jnp.mod(heading * (plane - z), planes)
            mine, other = sums[0]
            for j in range(1, planes):
                mine = jnp.where(at == j, sums[j][0], mine)
                other = jnp.where(at == j, sums[j][1], other)
            placed += [jnp.where(y == 0, mine, other), jnp.where(y == 0, other, mine)]
        return jnp.concatenate(placed, axis=0)

    for step in plan(planes):
        stream, move, j = step
        if move == "mul":
            multiply_exported(j) if stream == "x" else multiply(stream, j)
        elif move == "back":
            back = send(have["x", "far", 0], outward)
        elif move == "f":
            strips = [factor_band[:, left : left + sizes["x"] * LANE] for _, left in starts_of("x")]
            have[step] = send(jnp.concatenate(strips, axis=0), inward)
        elif move == "sel":
            have[stream, "slot", j] = choose(j <= reach, have[stream, "e", j], have[stream, "m", planes - j])
        elif step == ("bx", "y", 0):
            have["bx", "slot", 0] = jnp.concatenate([own["bx"], send(own["bx"], side)], axis=0)
            for part in ("b", "x"):
                if part in sizes:
                    have[part, "slot", 0] = cut(part, have["bx", "slot", 0])
        elif move == "y":
            have[step] = send(have[stream, "slot", j], side)
        else:
            came = have[stream, "m" if move == "e" else "e", j - 1] if j > 1 else have[stream, "slot", 0]
            pairs = odd if move == "m" else inward if stream == "x" else even
            if exports(planes) and move == "e" and j > 1:
                pairs = outward
            have[step] = send(came, pairs)
            if stream == "bx":
                for part in ("b", "x"):
                    have[part, move, j] = cut(part, have[step])
            if move == "e" and j == 1:
                have[stream, "slot", 1] = have[step]

    total = place([[sum(terms) for terms in pair] for pair in parts])
    if exports(planes):
        total = total + jnp.where(outer, back, 0.0)
    share = rows * row_size // col_size
    total = total.reshape(col_size, share, band)

    samples = lax.dynamic_index_in_dim(total, col, 0, keepdims=False)
    for k in range(1, col_size):
        pairs = [(c, c ^ k) for c in range(col_size)]
        samples = samples + lax.ppermute(lax.dynamic_index_in_dim(total, col ^ k, 0, keepdims=False), "col", pairs)

    speed = site_mean[None, :] + site_spread[None, :] * samples
    positive = jnp.maximum(speed, 0.0)
    wind = jnp.clip((positive * positive * positive - 27.0) / (1728.0 - 27.0), 0.0, 1.0)
    solar = jnp.clip(speed / 12.0, 0.0, 1.0)
    power = jnp.where(site_kind[None, :] == 1, solar, wind) * site_capacity[None, :]

    power = jnp.concatenate([power, site_plant[None, :].astype(jnp.float32)], axis=0)
    pair = jnp.concatenate([power, send(power, side)], axis=1)
    table = jnp.concatenate(
        [pair] + [send(pair, line(lambda p, k=k: p ^ k)) for k in range(1, planes)], axis=1
    )
    plant = table[share].astype(jnp.int32)
    mine = PLANTS // row_size
    onehot = (plant[:, None] == row * mine + jnp.arange(mine, dtype=jnp.int32)[None, :]).astype(jnp.float32)
    return jnp.dot(table[:share], onehot, precision=lax.Precision.HIGHEST, preferred_element_type=jnp.float32)


def solution(mesh):
    in_specs = (P("row", "col"), P("col", "row"), P("row"), P("row"), P("row"), P("row"), P("row"))
    out_specs = P("col", "row")
    return jax.shard_map(body, mesh=mesh, in_specs=in_specs, out_specs=out_specs, check_vma=False)
```

```python
import math

import jax
import jax.numpy as jnp
from jax import lax
from jax.experimental import pallas as pl
from jax.experimental.pallas import tpu as pltpu
from jax.sharding import PartitionSpec as P


PLANTS = 2048
LANE = 128


def split_bf16(x):
    hi = x.astype(jnp.bfloat16)
    return hi, (x - hi.astype(jnp.float32)).astype(jnp.bfloat16)


def dot_t(a, b):
    return lax.dot_general(a, b, (((1,), (1,)), ((), ())), preferred_element_type=jnp.float32)


def step_width(width):
    tiles = width // LANE
    return LANE * max(d for d in range(1, 29) if tiles % d == 0 and (d < tiles or tiles == 1))


def products(blocks, factors, starts, rows, band, order=None):
    folds = len(factors)
    arrays, specs, flags, places = [], [], [], []
    width = (blocks[0][1] if isinstance(blocks[0], tuple) else blocks[0]).shape[1]
    tk = step_width(width)
    steps = width // tk
    total = 0
    for block in blocks:
        if isinstance(block, tuple):
            flag, a, b = block
            k = len(flags)
            flags.append(flag)
            places.append((len(arrays), k))
            arrays += [a, b]
            specs.append(pl.BlockSpec((a.shape[0], tk), lambda i, *s, k=k: (0, i * s[k][0])))
            specs.append(pl.BlockSpec((a.shape[0], tk), lambda i, *s, k=k: (0, i * (1 - s[k][0]))))
        else:
            a = block
            places.append((len(arrays), None))
            arrays.append(a)
            specs.append(pl.BlockSpec((a.shape[0], tk), lambda i, *s: (0, i)))
        total += a.shape[0]
    groups = total // (folds * rows)
    scalars = flags + ([] if order is None else [order])

    for fold in range(folds):
        top, left = starts[fold]
        specs.append(
            pl.BlockSpec(
                (pl.Element(band), pl.Element(tk)),
                lambda i, *s, top=top, left=left: (top, pl.multiple_of(left + i * tk, LANE)),
            )
        )

    lows = [fold * rows // 8 * 8 for fold in range(folds)]
    tall = max(-(-(fold + 1) * rows // 8) * 8 - lows[fold] for fold in range(folds))
    lows = [min(low, folds * rows - tall) for low in lows]

    def kernel(*refs):
        scalar_refs, refs = refs[: len(scalars)], refs[len(scalars) :]
        out_ref, acc = refs[-2], refs[-1]
        factor_refs = refs[len(arrays) : len(arrays) + folds]
        step = pl.program_id(0)

        @pl.when(step == 0)
        def _():
            acc[...] = jnp.zeros_like(acc)

        taken = []
        for i, k in places:
            block = refs[i][...]
            if k is not None:
                block = jnp.where(scalar_refs[k][0] == 1, block, refs[i + 1][...])
            taken += [block[top : top + folds * rows] for top in range(0, block.shape[0], folds * rows)]
        for fold in range(folds):
            hi, lo = split_bf16(jnp.concatenate([t[lows[fold] : lows[fold] + tall] for t in taken], axis=0))
            f_hi, f_lo = split_bf16(factor_refs[fold][...])
            first = dot_t(jnp.concatenate([hi, lo], axis=0), f_hi)
            acc[fold] += first[: groups * tall] + (first[groups * tall :] + dot_t(hi, f_lo))

        @pl.when(step == steps - 1)
        def _():
            for g in range(groups):
                base = [g * tall + fold * rows - lows[fold] for fold in range(folds)]
                out_ref[g if order is None else scalar_refs[-1][g]] = sum(
                    acc[fold, base[fold] : base[fold] + rows] for fold in range(folds)
                )

    return pl.pallas_call(
        kernel,
        grid_spec=pltpu.PrefetchScalarGridSpec(
            num_scalar_prefetch=len(scalars),
            grid=(steps,),
            in_specs=specs,
            out_specs=pl.BlockSpec((groups, rows, band), lambda i, *s: (0, 0, 0)),
            scratch_shapes=[pltpu.VMEM((folds, groups * tall, band), jnp.float32)],
        ),
        out_shape=jax.ShapeDtypeStruct((groups, rows, band), jnp.float32),
    )(*scalars, *arrays, *factors)


CHUNKS = 2


def choose(flag, a, b):
    height, width = a.shape
    tk = step_width(width)

    def kernel(flag_ref, a_ref, b_ref, out_ref):
        @pl.when(flag_ref[0] == 1)
        def _():
            out_ref[...] = a_ref[...]

        @pl.when(flag_ref[0] != 1)
        def _():
            out_ref[...] = b_ref[...]

    return pl.pallas_call(
        kernel,
        grid_spec=pltpu.PrefetchScalarGridSpec(
            num_scalar_prefetch=1,
            grid=(width // tk,),
            in_specs=[
                pl.BlockSpec((height, tk), lambda i, flag: (0, i * flag[0])),
                pl.BlockSpec((height, tk), lambda i, flag: (0, i * (1 - flag[0]))),
            ],
            out_specs=pl.BlockSpec((height, tk), lambda i, flag: (0, i)),
        ),
        out_shape=jax.ShapeDtypeStruct(a.shape, a.dtype),
    )(flag, a, b)


def arriving(t, planes):
    if t == 1:
        return [1]
    return sorted({t, planes - t} - {1}) if 2 * t >= planes else []


def exports(planes):
    return planes == 4


def plan(planes):
    slots = lambda *js: tuple(("slot", j) for j in js)
    if exports(planes):
        near = slots(0) + (("y", 0),) + slots(1)
        inner = (("y", 1),) + slots(2) + (("y", 2),) + slots(3)
        return (
            [("bx", "y", 0), ("0", "e", 1), ("0", "m", 1), ("1", "e", 1), ("0", "y", 0), ("1", "m", 1), ("1", "y", 0)]
            + [("b", "e", 1), ("x", "e", 1), ("x", "f", 0)]
            + [("0", "y", 1), ("0", "m", 2), ("0", "e", 2), ("0", "mul", near)]
            + [("1", "y", 1), ("1", "m", 2), ("1", "e", 2), ("bx", "m", 1), ("1", "mul", near)]
            + [("b", "m", 2), ("x", "m", 2), ("b", "mul", slots(0, 1))]
            + [("0", "sel", 2), ("0", "y", 2), ("0", "e", 3)]
            + [("1", "sel", 2), ("1", "y", 2), ("1", "e", 3), ("b", "e", 2)]
            + [("0", "sel", 3), ("0", "y", 3), ("0", "mul", inner)]
            + [("1", "sel", 3), ("1", "y", 3), ("b", "e", 3), ("1", "mul", inner)]
            + [("x", "mul", "own"), ("x", "mul", "far"), ("x", "back", 0)]
            + [("0", "mul", (("y", 3),)), ("b", "mul", slots(2, 3)), ("1", "mul", (("y", 3),))]
        )
    chunks = [str(c) for c in range(CHUNKS)]
    last = planes - 1
    steps = [("bx", "y", 0)]
    for c in chunks:
        steps += [(c, "e", 1), (c, "y", 0)] + [(c, "m", 1)] * (last > 1)
    steps += [("b", "e", 1)] + [("b", "m", 1)] * (last > 1)
    steps += [(c, "mul", slots(0)) for c in chunks]
    sent = [0]
    for t in range(1, planes):
        new = arriving(t, planes)
        if t == last:
            for j in range(2, planes):
                steps += [("b", "e", j)] + [("b", "m", j + 1)] * (1 < j < last - 1)
        for c in chunks:
            for j in new:
                steps += [(c, "sel", j)] * (j > 1) + [(c, "y", j)]
            if t < last:
                steps += [(c, "m", t + 1)] * (t + 1 < last) + [(c, "e", t + 1)]
            if t == 1 and c == chunks[-1] and last > 2:
                steps += [("b", "m", 2)]
            if sent or new:
                steps += [(c, "mul", tuple(("y", j) for j in sent) + slots(*new))]
        if t == 1:
            steps += [("b", "mul", slots(0, 1))]
        sent = new
    for t in range(2, last):
        if arriving(t, planes):
            steps += [("b", "mul", slots(*arriving(t, planes)))]
    steps += [(c, "mul", tuple(("y", j) for j in sent)) for c in chunks[:-1]]
    if last > 1:
        steps += [("b", "mul", slots(last))]
    steps += [(c, "mul", tuple(("y", j) for j in sent)) for c in chunks[-1:]]
    return steps


def body(factor_band, normals, site_mean, site_spread, site_capacity, site_kind, site_plant):
    row_size, col_size = lax.axis_size("row"), lax.axis_size("col")
    row, col = lax.axis_index("row"), lax.axis_index("col")
    planes = row_size // 2
    z, y = row // 2, row % 2
    cols, rows = normals.shape
    band = factor_band.shape[0]
    folds = 8 // math.gcd(rows, 8)
    stride = cols // folds

    side = [(r, r ^ 1) for r in range(row_size)]

    def line(neighbour):
        return [(r, 2 * neighbour(r // 2) + r % 2) for r in range(row_size)]

    even = line(lambda p: p ^ 1)
    odd = [pair for pair in line(lambda p: ((p - 1) ^ 1) + 1) if pair[0] // 2 not in (0, planes - 1)]
    send = lambda x, pairs: lax.ppermute(x, "row", pairs)
    heading = 1 - 2 * (z % 2)
    reach = jnp.where(heading == 1, planes - 1 - z, z)

    near_end = [(j <= reach).astype(jnp.int32).reshape(1) for j in range(planes)]
    outer = (z == 0) | (z == planes - 1)

    def between(pairs, take):
        return [(a, b) for a, b in pairs if take(a // 2 in (0, planes - 1))]

    inward = between(even, lambda is_outer: is_outer)
    outward = between(even, lambda is_outer: not is_outer)

    turned = normals.T
    tiles = stride // LANE
    pairs_of = lambda share: 2 * round(tiles * share / 2)
    sizes = {"x": pairs_of(18 / 128), "b": pairs_of(22 / 128)} if exports(planes) else {"b": pairs_of(20 / 128)}
    rest = tiles - sum(sizes.values())
    sizes["1"] = 2 * (rest * 5 // 22)
    sizes["0"] = rest - sizes["1"]
    begin, at = {}, 0
    for stream in sizes:
        begin[stream], at = at * LANE, at + sizes[stream]

    begin["bx"], sizes["bx"] = 0, sizes["b"] + sizes.get("x", 0)

    def piece(stream):
        start, width = begin[stream], sizes[stream] * LANE
        return jnp.concatenate(
            [turned[:, f * stride + start : f * stride + start + width] for f in range(folds)], axis=0
        )

    own = {stream: piece(stream) for stream in ("bx", "0", "1")}
    have = {(stream, "slot", 0): own[stream] for stream in ("0", "1")}
    parts = [[[], []] for _ in range(planes)]

    def starts_of(stream):
        return [(0, f * stride + begin[stream]) for f in range(folds)]

    def cut(stream, block):
        return block[:, begin[stream] : begin[stream] + sizes[stream] * LANE]

    def multiply(stream, wanted):
        blocks, places = [], []
        for kind, j in wanted:
            if stream == "b" and j > 1:
                blocks.append((near_end[j], have["b", "e", j], have["b", "m", planes - j]))
            else:
                blocks.append(have[stream, kind, j])
            places += [(j, 0), (j, 1)] if stream == "b" else [(j, int(kind == "y"))]
        got = products(blocks, [factor_band] * folds, starts_of(stream), rows, band)
        for g, (j, q) in enumerate(places):
            parts[j][q].append(got[g])

    def multiply_exported(whose):
        blocks = [have["x", "slot", 0], have["x", "e", 1], have["x", "m", 1], have["x", "m", 2]]
        places = [(j % planes, q) for j in (0, 1, -1, -2) for q in (0, 1)]
        if whose == "own":
            got = products(blocks, [factor_band] * folds, starts_of("x"), rows, band)
            for g, (j, q) in enumerate(places):
                parts[j][q].append(jnp.where(outer, 0.0, got[g]))
        else:
            slot, other = jnp.array(places, jnp.int32).T
            order = 2 * jnp.mod(z + heading * slot, planes) + (y + other) % 2
            have["x", "far", 0] = products(
                blocks, [have["x", "f", 0]] * folds, [(f * band, 0) for f in range(folds)], rows, band, order
            ).reshape(row_size * rows, band)

    def place(sums):
        placed = []
        for plane in range(planes):
            at = jnp.mod(heading * (plane - z), planes)
            mine, other = sums[0]
            for j in range(1, planes):
                mine = jnp.where(at == j, sums[j][0], mine)
                other = jnp.where(at == j, sums[j][1], other)
            placed += [jnp.where(y == 0, mine, other), jnp.where(y == 0, other, mine)]
        return jnp.concatenate(placed, axis=0)

    for step in plan(planes):
        stream, move, j = step
        if move == "mul":
            multiply_exported(j) if stream == "x" else multiply(stream, j)
        elif move == "back":
            back = send(have["x", "far", 0], outward)
        elif move == "f":
            strips = [factor_band[:, left : left + sizes["x"] * LANE] for _, left in starts_of("x")]
            have[step] = send(jnp.concatenate(strips, axis=0), inward)
        elif move == "sel":
            have[stream, "slot", j] = choose(near_end[j], have[stream, "e", j], have[stream, "m", planes - j])
        elif step == ("bx", "y", 0):
            have["bx", "slot", 0] = jnp.concatenate([own["bx"], send(own["bx"], side)], axis=0)
            for part in ("b", "x"):
                if part in sizes:
                    have[part, "slot", 0] = cut(part, have["bx", "slot", 0])
        elif move == "y":
            have[step] = send(have[stream, "slot", j], side)
        else:
            came = have[stream, "m" if move == "e" else "e", j - 1] if j > 1 else have[stream, "slot", 0]
            pairs = odd if move == "m" else inward if stream == "x" else even
            if exports(planes) and move == "e" and j > 1:
                pairs = outward
            have[step] = send(came, pairs)
            if stream == "bx":
                for part in ("b", "x"):
                    have[part, move, j] = cut(part, have[step])
            if move == "e" and j == 1:
                have[stream, "slot", 1] = have[step]

    total = place([[sum(terms) for terms in pair] for pair in parts])
    if exports(planes):
        total = total + jnp.where(outer, back, 0.0)
    share = rows * row_size // col_size
    total = total.reshape(col_size, share, band)

    samples = lax.dynamic_index_in_dim(total, col, 0, keepdims=False)
    for k in range(1, col_size):
        pairs = [(c, c ^ k) for c in range(col_size)]
        samples = samples + lax.ppermute(lax.dynamic_index_in_dim(total, col ^ k, 0, keepdims=False), "col", pairs)

    speed = site_mean[None, :] + site_spread[None, :] * samples
    positive = jnp.maximum(speed, 0.0)
    wind = jnp.clip((positive * positive * positive - 27.0) / (1728.0 - 27.0), 0.0, 1.0)
    solar = jnp.clip(speed / 12.0, 0.0, 1.0)
    power = jnp.where(site_kind[None, :] == 1, solar, wind) * site_capacity[None, :]

    power = jnp.concatenate([power, site_plant[None, :].astype(jnp.float32)], axis=0)
    pair = jnp.concatenate([power, send(power, side)], axis=1)
    table = jnp.concatenate(
        [pair] + [send(pair, line(lambda p, k=k: p ^ k)) for k in range(1, planes)], axis=1
    )
    plant = table[share].astype(jnp.int32)
    mine = PLANTS // row_size
    onehot = (plant[:, None] == row * mine + jnp.arange(mine, dtype=jnp.int32)[None, :]).astype(jnp.float32)
    return jnp.dot(table[:share], onehot, precision=lax.Precision.HIGHEST, preferred_element_type=jnp.float32)


def solution(mesh):
    in_specs = (P("row", "col"), P("col", "row"), P("row"), P("row"), P("row"), P("row"), P("row"))
    out_specs = P("col", "row")
    return jax.shard_map(body, mesh=mesh, in_specs=in_specs, out_specs=out_specs, check_vma=False)
```

```python
import math

import jax
import jax.numpy as jnp
from jax import lax
from jax.experimental import pallas as pl
from jax.experimental.pallas import tpu as pltpu
from jax.sharding import PartitionSpec as P


PLANTS = 2048
LANE = 128


def split_bf16(x):
    hi = x.astype(jnp.bfloat16)
    return hi, (x - hi.astype(jnp.float32)).astype(jnp.bfloat16)


def dot_t(a, b):
    return lax.dot_general(a, b, (((1,), (1,)), ((), ())), preferred_element_type=jnp.float32)


def step_width(width):
    tiles = width // LANE
    return LANE * max(d for d in range(1, 29) if tiles % d == 0 and (d < tiles or tiles == 1))


def products(blocks, factors, starts, rows, band, width, order=None, resident=False):
    folds = len(factors)
    arrays, specs, flags, places = [], [], [], []
    tk = step_width(width)
    steps = width // tk
    total = 0
    for block in blocks:
        if isinstance(block, tuple):
            flag, a, b = block
            k = len(flags)
            flags.append(flag)
            places.append((len(arrays), k))
            arrays += [a, b]
            specs.append(pl.BlockSpec((a.shape[0], tk), lambda i, *s, k=k: (0, i * s[k][0])))
            specs.append(pl.BlockSpec((a.shape[0], tk), lambda i, *s, k=k: (0, i * (1 - s[k][0]))))
        else:
            a = block
            places.append((len(arrays), None))
            arrays.append(a)
            specs.append(pl.BlockSpec((a.shape[0], tk), lambda i, *s: (0, i)))
        total += a.shape[0]
    groups = total // (folds * rows)
    scalars = flags + ([] if order is None else [order])

    if resident:
        specs.append(pl.BlockSpec(memory_space=pltpu.VMEM))
        factors = factors[:1]
    for fold in range(0 if resident else folds):
        top, left = starts[fold]
        specs.append(
            pl.BlockSpec(
                (pl.Element(band), pl.Element(tk)),
                lambda i, *s, top=top, left=left: (top, pl.multiple_of(left + i * tk, LANE)),
            )
        )

    lows = [fold * rows // 8 * 8 for fold in range(folds)]
    tall = max(-(-(fold + 1) * rows // 8) * 8 - lows[fold] for fold in range(folds))
    lows = [min(low, folds * rows - tall) for low in lows]

    def kernel(*refs):
        scalar_refs, refs = refs[: len(scalars)], refs[len(scalars) :]
        out_ref, acc = refs[-2], refs[-1]
        factor_refs = refs[len(arrays) : len(arrays) + folds]
        step = pl.program_id(0)

        @pl.when(step == 0)
        def _():
            acc[...] = jnp.zeros_like(acc)

        taken = []
        for i, k in places:
            block = refs[i][...]
            if k is not None:
                block = jnp.where(scalar_refs[k][0] == 1, block, refs[i + 1][...])
            taken += [block[top : top + folds * rows] for top in range(0, block.shape[0], folds * rows)]
        for fold in range(folds):
            hi, lo = split_bf16(jnp.concatenate([t[lows[fold] : lows[fold] + tall] for t in taken], axis=0))
            if resident:
                top, left = starts[fold]
                strip = factor_refs[0][top : top + band, pl.ds(pl.multiple_of(left + step * tk, LANE), tk)]
            else:
                strip = factor_refs[fold][...]
            f_hi, f_lo = split_bf16(strip)
            first = dot_t(jnp.concatenate([hi, lo], axis=0), f_hi)
            acc[fold] += first[: groups * tall] + (first[groups * tall :] + dot_t(hi, f_lo))

        @pl.when(step == steps - 1)
        def _():
            for g in range(groups):
                base = [g * tall + fold * rows - lows[fold] for fold in range(folds)]
                out_ref[g if order is None else scalar_refs[-1][g]] = sum(
                    acc[fold, base[fold] : base[fold] + rows] for fold in range(folds)
                )

    return pl.pallas_call(
        kernel,
        grid_spec=pltpu.PrefetchScalarGridSpec(
            num_scalar_prefetch=len(scalars),
            grid=(steps,),
            in_specs=specs,
            out_specs=pl.BlockSpec((groups, rows, band), lambda i, *s: (0, 0, 0)),
            scratch_shapes=[pltpu.VMEM((folds, groups * tall, band), jnp.float32)],
        ),
        out_shape=jax.ShapeDtypeStruct((groups, rows, band), jnp.float32),
    )(*scalars, *arrays, *factors)


CHUNKS = 2


def choose(flag, a, b):
    height, width = a.shape
    tk = step_width(width)

    def kernel(flag_ref, a_ref, b_ref, out_ref):
        @pl.when(flag_ref[0] == 1)
        def _():
            out_ref[...] = a_ref[...]

        @pl.when(flag_ref[0] != 1)
        def _():
            out_ref[...] = b_ref[...]

    return pl.pallas_call(
        kernel,
        grid_spec=pltpu.PrefetchScalarGridSpec(
            num_scalar_prefetch=1,
            grid=(width // tk,),
            in_specs=[
                pl.BlockSpec((height, tk), lambda i, flag: (0, i * flag[0])),
                pl.BlockSpec((height, tk), lambda i, flag: (0, i * (1 - flag[0]))),
            ],
            out_specs=pl.BlockSpec((height, tk), lambda i, flag: (0, i)),
        ),
        out_shape=jax.ShapeDtypeStruct(a.shape, a.dtype),
    )(flag, a, b)


def arriving(t, planes):
    if t == 1:
        return [1]
    return sorted({t, planes - t} - {1}) if 2 * t >= planes else []


def exports(planes):
    return planes == 4


def plan(planes):
    slots = lambda *js: tuple(("slot", j) for j in js)
    if exports(planes):
        near = slots(0) + (("y", 0),) + slots(1)
        inner = (("y", 1),) + slots(2) + (("y", 2),) + slots(3)
        return (
            [("0", "e", 1), ("0", "m", 1), ("bx", "y", 0), ("1", "e", 1), ("0", "y", 0), ("1", "m", 1), ("1", "y", 0)]
            + [("b", "e", 1), ("x", "e", 1), ("x", "f", 0)]
            + [("0", "y", 1), ("0", "m", 2), ("0", "e", 2), ("0", "mul", near)]
            + [("1", "y", 1), ("1", "m", 2), ("1", "e", 2), ("bx", "m", 1), ("1", "mul", near)]
            + [("x", "m", 2), ("b", "m", 2)]
            + [("0", "sel", 2), ("0", "y", 2), ("0", "e", 3)]
            + [("1", "sel", 2), ("1", "y", 2), ("1", "e", 3), ("b", "mul", slots(0, 1)), ("b", "e", 2)]
            + [("0", "sel", 3), ("0", "y", 3), ("0", "mul", inner), ("x", "mul", "own")]
            + [("1", "sel", 3), ("1", "y", 3), ("b", "e", 3)]
            + [("x", "mul", "far"), ("x", "back", 0), ("0", "mul", (("y", 3),)), ("b", "mul", slots(2, 3))]
            + [("1", "mul", inner + (("y", 3),))]
        )
    chunks = [str(c) for c in range(CHUNKS)]
    last = planes - 1
    steps = [("bx", "y", 0)]
    for c in chunks:
        steps += [(c, "e", 1), (c, "y", 0)] + [(c, "m", 1)] * (last > 1)
    steps += [("b", "e", 1)] + [("b", "m", 1)] * (last > 1)
    steps += [(c, "mul", slots(0)) for c in chunks]
    sent = [0]
    for t in range(1, planes):
        new = arriving(t, planes)
        if t == last:
            for j in range(2, planes):
                steps += [("b", "e", j)] + [("b", "m", j + 1)] * (1 < j < last - 1)
        for c in chunks:
            for j in new:
                steps += [(c, "sel", j)] * (j > 1) + [(c, "y", j)]
            if t < last:
                steps += [(c, "m", t + 1)] * (t + 1 < last) + [(c, "e", t + 1)]
            if t == 1 and c == chunks[-1] and last > 2:
                steps += [("b", "m", 2)]
            if sent or new:
                steps += [(c, "mul", tuple(("y", j) for j in sent) + slots(*new))]
        if t == 1:
            steps += [("b", "mul", slots(0, 1))]
        sent = new
    for t in range(2, last):
        if arriving(t, planes):
            steps += [("b", "mul", slots(*arriving(t, planes)))]
    steps += [(c, "mul", tuple(("y", j) for j in sent)) for c in chunks[:-1]]
    if last > 1:
        steps += [("b", "mul", slots(last))]
    steps += [(c, "mul", tuple(("y", j) for j in sent)) for c in chunks[-1:]]
    return steps


def body(factor_band, normals, site_mean, site_spread, site_capacity, site_kind, site_plant):
    row_size, col_size = lax.axis_size("row"), lax.axis_size("col")
    row, col = lax.axis_index("row"), lax.axis_index("col")
    planes = row_size // 2
    z, y = row // 2, row % 2
    cols, rows = normals.shape
    band = factor_band.shape[0]
    folds = 8 // math.gcd(rows, 8)
    stride = cols // folds

    side = [(r, r ^ 1) for r in range(row_size)]

    def line(neighbour):
        return [(r, 2 * neighbour(r // 2) + r % 2) for r in range(row_size)]

    even = line(lambda p: p ^ 1)
    odd = [pair for pair in line(lambda p: ((p - 1) ^ 1) + 1) if pair[0] // 2 not in (0, planes - 1)]
    send = lambda x, pairs: lax.ppermute(x, "row", pairs)
    heading = 1 - 2 * (z % 2)
    reach = jnp.where(heading == 1, planes - 1 - z, z)

    near_end = [(j <= reach).astype(jnp.int32).reshape(1) for j in range(planes)]
    outer = (z == 0) | (z == planes - 1)

    def between(pairs, take):
        return [(a, b) for a, b in pairs if take(a // 2 in (0, planes - 1))]

    inward = between(even, lambda is_outer: is_outer)
    outward = between(even, lambda is_outer: not is_outer)

    turned = normals.T
    tiles = stride // LANE
    pairs_of = lambda share: 2 * round(tiles * share / 2)
    sizes = {"x": pairs_of(18 / 128), "b": pairs_of(22 / 128)} if exports(planes) else {"b": pairs_of(20 / 128)}
    rest = tiles - sum(sizes.values())
    sizes["1"] = 2 * (rest * 9 // 44)
    sizes["0"] = rest - sizes["1"]
    begin, at = {}, 0
    for stream in sizes:
        begin[stream], at = at * LANE, at + sizes[stream]

    begin["bx"], sizes["bx"] = 0, sizes["b"] + sizes.get("x", 0)

    def piece(stream):
        start, width = begin[stream], sizes[stream] * LANE
        return jnp.concatenate(
            [turned[:, f * stride + start : f * stride + start + width] for f in range(folds)], axis=0
        )

    own = {stream: piece(stream) for stream in ("0", "bx", "1")}
    have = {(stream, "slot", 0): own[stream] for stream in ("0", "1")}
    parts = [[[], []] for _ in range(planes)]

    def starts_of(stream):
        return [(0, f * stride + begin[stream]) for f in range(folds)]

    def cut(stream, block):
        return block[:, begin[stream] : begin[stream] + sizes[stream] * LANE]

    def multiply(stream, wanted):
        blocks, places = [], []
        for kind, j in wanted:
            if stream == "b" and j > 1:
                blocks.append((near_end[j], have["b", "e", j], have["b", "m", planes - j]))
            else:
                blocks.append(have[stream, kind, j])
            places += [(j, 0), (j, 1)] if stream == "b" else [(j, int(kind == "y"))]
        got = products(blocks, [factor_band] * folds, starts_of(stream), rows, band, sizes[stream] * LANE)
        for g, (j, q) in enumerate(places):
            parts[j][q].append(got[g])

    def multiply_exported(whose):
        blocks = [have["x", "slot", 0], have["x", "e", 1], have["bx", "m", 1], have["x", "m", 2]]
        places = [(j % planes, q) for j in (0, 1, -1, -2) for q in (0, 1)]
        slot, other = jnp.array(places, jnp.int32).T
        order = 2 * jnp.mod(z + heading * slot, planes) + (y + other) % 2
        factors, starts = [factor_band] * folds, starts_of("x")
        if whose == "far":
            factors, starts = [have["x", "f", 0]] * folds, [(f * band, 0) for f in range(folds)]
        sums = products(blocks, factors, starts, rows, band, sizes["x"] * LANE, order, whose == "far")
        have["x", whose, 0] = sums.reshape(row_size * rows, band)

    def place(sums):
        placed = []
        for plane in range(planes):
            at = jnp.mod(heading * (plane - z), planes)
            mine, other = sums[0]
            for j in range(1, planes):
                mine = jnp.where(at == j, sums[j][0], mine)
                other = jnp.where(at == j, sums[j][1], other)
            placed += [jnp.where(y == 0, mine, other), jnp.where(y == 0, other, mine)]
        return jnp.concatenate(placed, axis=0)

    for step in plan(planes):
        stream, move, j = step
        if move == "mul":
            multiply_exported(j) if stream == "x" else multiply(stream, j)
        elif move == "back":
            back = send(have["x", "far", 0], outward)
        elif move == "f":
            strips = [factor_band[:, left : left + sizes["x"] * LANE] for _, left in starts_of("x")]
            have[step] = send(jnp.concatenate(strips, axis=0), inward)
        elif move == "sel":
            have[stream, "slot", j] = choose(near_end[j], have[stream, "e", j], have[stream, "m", planes - j])
        elif step == ("bx", "y", 0):
            have["bx", "slot", 0] = jnp.concatenate([own["bx"], send(own["bx"], side)], axis=0)
            for part in ("b", "x"):
                if part in sizes:
                    have[part, "slot", 0] = cut(part, have["bx", "slot", 0])
        elif move == "y":
            have[step] = send(have[stream, "slot", j], side)
        else:
            came = have[stream, "m" if move == "e" else "e", j - 1] if j > 1 else have[stream, "slot", 0]
            pairs = odd if move == "m" else inward if stream == "x" else even
            if exports(planes) and move == "e" and j > 1:
                pairs = outward
            have[step] = send(came, pairs)
            if stream == "bx":
                for part in ("b", "x"):
                    have[part, move, j] = cut(part, have[step])
            if move == "e" and j == 1:
                have[stream, "slot", 1] = have[step]

    total = place([[sum(terms) for terms in pair] for pair in parts])
    if exports(planes):
        total = total + jnp.where(outer, back, have["x", "own", 0])
    share = rows * row_size // col_size
    total = total.reshape(col_size, share, band)

    samples = lax.dynamic_index_in_dim(total, col, 0, keepdims=False)
    for k in range(1, col_size):
        pairs = [(c, c ^ k) for c in range(col_size)]
        samples = samples + lax.ppermute(lax.dynamic_index_in_dim(total, col ^ k, 0, keepdims=False), "col", pairs)

    speed = site_mean[None, :] + site_spread[None, :] * samples
    positive = jnp.maximum(speed, 0.0)
    wind = jnp.clip((positive * positive * positive - 27.0) / (1728.0 - 27.0), 0.0, 1.0)
    solar = jnp.clip(speed / 12.0, 0.0, 1.0)
    power = jnp.where(site_kind[None, :] == 1, solar, wind) * site_capacity[None, :]

    power = jnp.concatenate([power, site_plant[None, :].astype(jnp.float32)], axis=0)
    pair = jnp.concatenate([power, send(power, side)], axis=1)
    table = jnp.concatenate(
        [pair] + [send(pair, line(lambda p, k=k: p ^ k)) for k in range(1, planes)], axis=1
    )
    plant = table[share].astype(jnp.int32)
    mine = PLANTS // row_size
    onehot = (plant[:, None] == row * mine + jnp.arange(mine, dtype=jnp.int32)[None, :]).astype(jnp.float32)
    return jnp.dot(table[:share], onehot, precision=lax.Precision.HIGHEST, preferred_element_type=jnp.float32)


def solution(mesh):
    in_specs = (P("row", "col"), P("col", "row"), P("row"), P("row"), P("row"), P("row"), P("row"))
    out_specs = P("col", "row")
    return jax.shard_map(body, mesh=mesh, in_specs=in_specs, out_specs=out_specs, check_vma=False)
```

```python
import math

import jax
import jax.numpy as jnp
from jax import lax
from jax.experimental import pallas as pl
from jax.experimental.pallas import tpu as pltpu
from jax.sharding import PartitionSpec as P


PLANTS = 2048
LANE = 128


def split_bf16(x):
    hi = x.astype(jnp.bfloat16)
    return hi, (x - hi.astype(jnp.float32)).astype(jnp.bfloat16)


def dot_t(a, b):
    return lax.dot_general(a, b, (((1,), (1,)), ((), ())), preferred_element_type=jnp.float32)


def step_width(width):
    tiles = width // LANE
    return LANE * max(d for d in range(1, 29) if tiles % d == 0 and (d < tiles or tiles == 1))


def products(blocks, factors, starts, rows, band, width, order=None, resident=False):
    folds = len(factors)
    arrays, specs, flags, places = [], [], [], []
    tk = step_width(width)
    steps = width // tk
    total = 0
    for block in blocks:
        if isinstance(block, tuple):
            flag, a, b = block
            k = len(flags)
            flags.append(flag)
            places.append((len(arrays), k))
            arrays += [a, b]
            specs.append(pl.BlockSpec((a.shape[0], tk), lambda i, *s, k=k: (0, i * s[k][0])))
            specs.append(pl.BlockSpec((a.shape[0], tk), lambda i, *s, k=k: (0, i * (1 - s[k][0]))))
        else:
            a = block
            places.append((len(arrays), None))
            arrays.append(a)
            specs.append(pl.BlockSpec((a.shape[0], tk), lambda i, *s: (0, i)))
        total += a.shape[0]
    groups = total // (folds * rows)
    scalars = flags + ([] if order is None else [order])

    if resident:
        specs.append(pl.BlockSpec(memory_space=pltpu.VMEM))
        factors = factors[:1]
    for fold in range(0 if resident else folds):
        top, left = starts[fold]
        specs.append(
            pl.BlockSpec(
                (pl.Element(band), pl.Element(tk)),
                lambda i, *s, top=top, left=left: (top, pl.multiple_of(left + i * tk, LANE)),
            )
        )

    lows = [fold * rows // 8 * 8 for fold in range(folds)]
    tall = max(-(-(fold + 1) * rows // 8) * 8 - lows[fold] for fold in range(folds))
    lows = [min(low, folds * rows - tall) for low in lows]

    def kernel(*refs):
        scalar_refs, refs = refs[: len(scalars)], refs[len(scalars) :]
        out_ref, acc = refs[-2], refs[-1]
        factor_refs = refs[len(arrays) : len(arrays) + folds]
        step = pl.program_id(0)

        @pl.when(step == 0)
        def _():
            acc[...] = jnp.zeros_like(acc)

        taken = []
        for i, k in places:
            block = refs[i][...]
            if k is not None:
                block = jnp.where(scalar_refs[k][0] == 1, block, refs[i + 1][...])
            taken += [block[top : top + folds * rows] for top in range(0, block.shape[0], folds * rows)]
        for fold in range(folds):
            hi, lo = split_bf16(jnp.concatenate([t[lows[fold] : lows[fold] + tall] for t in taken], axis=0))
            if resident:
                top, left = starts[fold]
                strip = factor_refs[0][top : top + band, pl.ds(pl.multiple_of(left + step * tk, LANE), tk)]
            else:
                strip = factor_refs[fold][...]
            f_hi, f_lo = split_bf16(strip)
            first = dot_t(jnp.concatenate([hi, lo], axis=0), f_hi)
            acc[fold] += first[: groups * tall] + (first[groups * tall :] + dot_t(hi, f_lo))

        @pl.when(step == steps - 1)
        def _():
            for g in range(groups):
                base = [g * tall + fold * rows - lows[fold] for fold in range(folds)]
                out_ref[g if order is None else scalar_refs[-1][g]] = sum(
                    acc[fold, base[fold] : base[fold] + rows] for fold in range(folds)
                )

    return pl.pallas_call(
        kernel,
        grid_spec=pltpu.PrefetchScalarGridSpec(
            num_scalar_prefetch=len(scalars),
            grid=(steps,),
            in_specs=specs,
            out_specs=pl.BlockSpec((groups, rows, band), lambda i, *s: (0, 0, 0)),
            scratch_shapes=[pltpu.VMEM((folds, groups * tall, band), jnp.float32)],
        ),
        out_shape=jax.ShapeDtypeStruct((groups, rows, band), jnp.float32),
    )(*scalars, *arrays, *factors)


CHUNKS = 2


def choose(flag, a, b):
    height, width = a.shape
    tk = step_width(width)

    def kernel(flag_ref, a_ref, b_ref, out_ref):
        @pl.when(flag_ref[0] == 1)
        def _():
            out_ref[...] = a_ref[...]

        @pl.when(flag_ref[0] != 1)
        def _():
            out_ref[...] = b_ref[...]

    return pl.pallas_call(
        kernel,
        grid_spec=pltpu.PrefetchScalarGridSpec(
            num_scalar_prefetch=1,
            grid=(width // tk,),
            in_specs=[
                pl.BlockSpec((height, tk), lambda i, flag: (0, i * flag[0])),
                pl.BlockSpec((height, tk), lambda i, flag: (0, i * (1 - flag[0]))),
            ],
            out_specs=pl.BlockSpec((height, tk), lambda i, flag: (0, i)),
        ),
        out_shape=jax.ShapeDtypeStruct(a.shape, a.dtype),
    )(flag, a, b)


def arriving(t, planes):
    if t == 1:
        return [1]
    return sorted({t, planes - t} - {1}) if 2 * t >= planes else []


def exports(planes):
    return planes == 4


def plan(planes):
    slots = lambda *js: tuple(("slot", j) for j in js)
    if exports(planes):
        near = slots(0) + (("y", 0),) + slots(1)
        inner = (("y", 1),) + slots(2) + (("y", 2),) + slots(3)
        return (
            [("0", "e", 1), ("0", "m", 1), ("bx", "y", 0), ("1", "e", 1), ("0", "y", 0), ("1", "m", 1), ("1", "y", 0)]
            + [("b", "e", 1), ("x", "e", 1), ("x", "f", 0)]
            + [("0", "y", 1), ("0", "m", 2), ("0", "e", 2), ("0", "mul", near)]
            + [("1", "y", 1), ("1", "m", 2), ("1", "e", 2), ("bx", "m", 1), ("1", "mul", near)]
            + [("x", "m", 2), ("b", "m", 2)]
            + [("0", "sel", 2), ("0", "y", 2), ("0", "e", 3)]
            + [("1", "sel", 2), ("1", "y", 2), ("1", "e", 3), ("b", "mul", slots(0, 1))]
            + [("0", "mul", (("y", 1),) + slots(2)), ("b", "e", 2)]
            + [("0", "sel", 3), ("0", "y", 3), ("x", "mul", "own")]
            + [("1", "sel", 3), ("1", "y", 3), ("b", "e", 3)]
            + [("x", "mul", "far"), ("x", "back", 0), ("0", "mul", (("y", 2),) + slots(3) + (("y", 3),))]
            + [("1", "mul", inner + (("y", 3),)), ("b", "mul", slots(2, 3))]
        )
    chunks = [str(c) for c in range(CHUNKS)]
    last = planes - 1
    steps = [("bx", "y", 0)]
    for c in chunks:
        steps += [(c, "e", 1), (c, "y", 0)] + [(c, "m", 1)] * (last > 1)
    steps += [("b", "e", 1)] + [("b", "m", 1)] * (last > 1)
    steps += [(c, "mul", slots(0)) for c in chunks]
    sent = [0]
    for t in range(1, planes):
        new = arriving(t, planes)
        if t == last:
            for j in range(2, planes):
                steps += [("b", "e", j)] + [("b", "m", j + 1)] * (1 < j < last - 1)
        for c in chunks:
            for j in new:
                steps += [(c, "sel", j)] * (j > 1) + [(c, "y", j)]
            if t < last:
                steps += [(c, "m", t + 1)] * (t + 1 < last) + [(c, "e", t + 1)]
            if t == 1 and c == chunks[-1] and last > 2:
                steps += [("b", "m", 2)]
            if sent or new:
                steps += [(c, "mul", tuple(("y", j) for j in sent) + slots(*new))]
        if t == 1:
            steps += [("b", "mul", slots(0, 1))]
        sent = new
    for t in range(2, last):
        if arriving(t, planes):
            steps += [("b", "mul", slots(*arriving(t, planes)))]
    steps += [(c, "mul", tuple(("y", j) for j in sent)) for c in chunks[:-1]]
    if last > 1:
        steps += [("b", "mul", slots(last))]
    steps += [(c, "mul", tuple(("y", j) for j in sent)) for c in chunks[-1:]]
    return steps


def body(factor_band, normals, site_mean, site_spread, site_capacity, site_kind, site_plant):
    row_size, col_size = lax.axis_size("row"), lax.axis_size("col")
    row, col = lax.axis_index("row"), lax.axis_index("col")
    planes = row_size // 2
    z, y = row // 2, row % 2
    cols, rows = normals.shape
    band = factor_band.shape[0]
    folds = 8 // math.gcd(rows, 8)
    stride = cols // folds

    side = [(r, r ^ 1) for r in range(row_size)]

    def line(neighbour):
        return [(r, 2 * neighbour(r // 2) + r % 2) for r in range(row_size)]

    even = line(lambda p: p ^ 1)
    odd = [pair for pair in line(lambda p: ((p - 1) ^ 1) + 1) if pair[0] // 2 not in (0, planes - 1)]
    send = lambda x, pairs: lax.ppermute(x, "row", pairs)
    heading = 1 - 2 * (z % 2)
    reach = jnp.where(heading == 1, planes - 1 - z, z)

    near_end = [(j <= reach).astype(jnp.int32).reshape(1) for j in range(planes)]
    outer = (z == 0) | (z == planes - 1)

    def between(pairs, take):
        return [(a, b) for a, b in pairs if take(a // 2 in (0, planes - 1))]

    inward = between(even, lambda is_outer: is_outer)
    outward = between(even, lambda is_outer: not is_outer)

    turned = normals.T
    tiles = stride // LANE
    pairs_of = lambda share: 2 * round(tiles * share / 2)
    sizes = {"x": pairs_of(18 / 128), "b": pairs_of(22 / 128)} if exports(planes) else {"b": pairs_of(20 / 128)}
    rest = tiles - sum(sizes.values())
    sizes["1"] = 2 * (rest * 9 // 44)
    sizes["0"] = rest - sizes["1"]
    begin, at = {}, 0
    for stream in sizes:
        begin[stream], at = at * LANE, at + sizes[stream]

    begin["bx"], sizes["bx"] = 0, sizes["b"] + sizes.get("x", 0)

    def piece(stream):
        start, width = begin[stream], sizes[stream] * LANE
        return jnp.concatenate(
            [turned[:, f * stride + start : f * stride + start + width] for f in range(folds)], axis=0
        )

    own = {stream: piece(stream) for stream in ("0", "bx", "1")}
    have = {(stream, "slot", 0): own[stream] for stream in ("0", "1")}
    parts = [[[], []] for _ in range(planes)]

    def starts_of(stream):
        return [(0, f * stride + begin[stream]) for f in range(folds)]

    def cut(stream, block):
        return block[:, begin[stream] : begin[stream] + sizes[stream] * LANE]

    def multiply(stream, wanted):
        blocks, places = [], []
        for kind, j in wanted:
            if stream == "b" and j > 1:
                blocks.append((near_end[j], have["b", "e", j], have["b", "m", planes - j]))
            else:
                blocks.append(have[stream, kind, j])
            places += [(j, 0), (j, 1)] if stream == "b" else [(j, int(kind == "y"))]
        got = products(blocks, [factor_band] * folds, starts_of(stream), rows, band, sizes[stream] * LANE)
        for g, (j, q) in enumerate(places):
            parts[j][q].append(got[g])

    def multiply_exported(whose):
        blocks = [have["x", "slot", 0], have["x", "e", 1], have["bx", "m", 1], have["x", "m", 2]]
        places = [(j % planes, q) for j in (0, 1, -1, -2) for q in (0, 1)]
        slot, other = jnp.array(places, jnp.int32).T
        order = 2 * jnp.mod(z + heading * slot, planes) + (y + other) % 2
        factors, starts = [factor_band] * folds, starts_of("x")
        if whose == "far":
            factors, starts = [have["x", "f", 0]] * folds, [(f * band, 0) for f in range(folds)]
        sums = products(blocks, factors, starts, rows, band, sizes["x"] * LANE, order, whose == "far")
        have["x", whose, 0] = sums

    def place(sums):
        placed = []
        for plane in range(planes):
            at = jnp.mod(heading * (plane - z), planes)
            mine, other = sums[0]
            for j in range(1, planes):
                mine = jnp.where(at == j, sums[j][0], mine)
                other = jnp.where(at == j, sums[j][1], other)
            placed += [jnp.where(y == 0, mine, other), jnp.where(y == 0, other, mine)]
        return jnp.stack(placed)

    for step in plan(planes):
        stream, move, j = step
        if move == "mul":
            multiply_exported(j) if stream == "x" else multiply(stream, j)
        elif move == "back":
            back = send(have["x", "far", 0], outward)
        elif move == "f":
            strips = [factor_band[:, left : left + sizes["x"] * LANE] for _, left in starts_of("x")]
            have[step] = send(jnp.concatenate(strips, axis=0), inward)
        elif move == "sel":
            have[stream, "slot", j] = choose(near_end[j], have[stream, "e", j], have[stream, "m", planes - j])
        elif step == ("bx", "y", 0):
            have["bx", "slot", 0] = jnp.concatenate([own["bx"], send(own["bx"], side)], axis=0)
            for part in ("b", "x"):
                if part in sizes:
                    have[part, "slot", 0] = cut(part, have["bx", "slot", 0])
        elif move == "y":
            have[step] = send(have[stream, "slot", j], side)
        else:
            came = have[stream, "m" if move == "e" else "e", j - 1] if j > 1 else have[stream, "slot", 0]
            pairs = odd if move == "m" else inward if stream == "x" else even
            if exports(planes) and move == "e" and j > 1:
                pairs = outward
            have[step] = send(came, pairs)
            if stream == "bx":
                for part in ("b", "x"):
                    have[part, move, j] = cut(part, have[step])
            if move == "e" and j == 1:
                have[stream, "slot", 1] = have[step]

    total = place([[sum(terms) for terms in pair] for pair in parts])
    if exports(planes):
        total = total + jnp.where(outer, back, have["x", "own", 0])
    share = rows * row_size // col_size
    total = total.reshape(col_size, share, band)

    samples = lax.dynamic_index_in_dim(total, col, 0, keepdims=False)
    for k in range(1, col_size):
        pairs = [(c, c ^ k) for c in range(col_size)]
        samples = samples + lax.ppermute(lax.dynamic_index_in_dim(total, col ^ k, 0, keepdims=False), "col", pairs)

    speed = site_mean[None, :] + site_spread[None, :] * samples
    positive = jnp.maximum(speed, 0.0)
    wind = jnp.clip((positive * positive * positive - 27.0) / (1728.0 - 27.0), 0.0, 1.0)
    solar = jnp.clip(speed / 12.0, 0.0, 1.0)
    power = jnp.where(site_kind[None, :] == 1, solar, wind) * site_capacity[None, :]

    power = jnp.concatenate([power, site_plant[None, :].astype(jnp.float32)], axis=0)
    pair = jnp.concatenate([power, send(power, side)], axis=1)
    table = jnp.concatenate(
        [pair] + [send(pair, line(lambda p, k=k: p ^ k)) for k in range(1, planes)], axis=1
    )
    plant = table[share].astype(jnp.int32)
    mine = PLANTS // row_size
    onehot = (plant[:, None] == row * mine + jnp.arange(mine, dtype=jnp.int32)[None, :]).astype(jnp.float32)
    return jnp.dot(table[:share], onehot, precision=lax.Precision.HIGHEST, preferred_element_type=jnp.float32)


def solution(mesh):
    in_specs = (P("row", "col"), P("col", "row"), P("row"), P("row"), P("row"), P("row"), P("row"))
    out_specs = P("col", "row")
    return jax.shard_map(body, mesh=mesh, in_specs=in_specs, out_specs=out_specs, check_vma=False)
```

```python
import math

import jax
import jax.numpy as jnp
from jax import lax
from jax.experimental import pallas as pl
from jax.experimental.pallas import tpu as pltpu
from jax.sharding import PartitionSpec as P


PLANTS = 2048
LANE = 128


def split_bf16(x):
    hi = x.astype(jnp.bfloat16)
    return hi, (x - hi.astype(jnp.float32)).astype(jnp.bfloat16)


def dot_t(a, b):
    return lax.dot_general(a, b, (((1,), (1,)), ((), ())), preferred_element_type=jnp.float32)


def step_width(width):
    tiles = width // LANE
    return LANE * max(d for d in range(1, 29) if tiles % d == 0 and (d < tiles or tiles == 1))


def products(blocks, factors, starts, rows, band, width, order=None, resident=False, limit=None):
    folds = len(factors)
    arrays, specs, flags, places = [], [], [], []
    tk = step_width(width)
    steps = width // tk
    total = 0
    for block in blocks:
        if isinstance(block, tuple):
            flag, a, b = block
            k = len(flags)
            flags.append(flag)
            places.append((len(arrays), k))
            arrays += [a, b]
            specs.append(pl.BlockSpec((a.shape[0], tk), lambda i, *s, k=k: (0, i * s[k][0])))
            specs.append(pl.BlockSpec((a.shape[0], tk), lambda i, *s, k=k: (0, i * (1 - s[k][0]))))
        else:
            a = block
            places.append((len(arrays), None))
            arrays.append(a)
            specs.append(pl.BlockSpec((a.shape[0], tk), lambda i, *s: (0, i)))
        total += a.shape[0]
    groups = total // (folds * rows)
    scalars = flags + ([] if order is None else [order])

    if resident:
        specs.append(pl.BlockSpec(memory_space=pltpu.VMEM))
        factors = factors[:1]
    for fold in range(0 if resident else folds):
        top, left = starts[fold]
        specs.append(
            pl.BlockSpec(
                (pl.Element(band), pl.Element(tk)),
                lambda i, *s, top=top, left=left: (top, pl.multiple_of(left + i * tk, LANE)),
            )
        )

    lows = [fold * rows // 8 * 8 for fold in range(folds)]
    tall = max(-(-(fold + 1) * rows // 8) * 8 - lows[fold] for fold in range(folds))
    lows = [min(low, folds * rows - tall) for low in lows]

    def kernel(*refs):
        scalar_refs, refs = refs[: len(scalars)], refs[len(scalars) :]
        out_ref, acc = refs[-2], refs[-1]
        factor_refs = refs[len(arrays) : len(arrays) + folds]
        step = pl.program_id(0)

        @pl.when(step == 0)
        def _():
            acc[...] = jnp.zeros_like(acc)

        taken = []
        for i, k in places:
            block = refs[i][...]
            if k is not None:
                block = jnp.where(scalar_refs[k][0] == 1, block, refs[i + 1][...])
            taken += [block[top : top + folds * rows] for top in range(0, block.shape[0], folds * rows)]
        for fold in range(folds):
            hi, lo = split_bf16(jnp.concatenate([t[lows[fold] : lows[fold] + tall] for t in taken], axis=0))
            if resident:
                top, left = starts[fold]
                strip = factor_refs[0][top : top + band, pl.ds(pl.multiple_of(left + step * tk, LANE), tk)]
            else:
                strip = factor_refs[fold][...]
            f_hi, f_lo = split_bf16(strip)
            first = dot_t(jnp.concatenate([hi, lo], axis=0), f_hi)
            acc[fold] += first[: groups * tall] + (first[groups * tall :] + dot_t(hi, f_lo))

        @pl.when(step == steps - 1)
        def _():
            for g in range(groups):
                base = [g * tall + fold * rows - lows[fold] for fold in range(folds)]
                out_ref[g if order is None else scalar_refs[-1][g]] = sum(
                    acc[fold, base[fold] : base[fold] + rows] for fold in range(folds)
                )

    return pl.pallas_call(
        kernel,
        grid_spec=pltpu.PrefetchScalarGridSpec(
            num_scalar_prefetch=len(scalars),
            grid=(steps,),
            in_specs=specs,
            out_specs=pl.BlockSpec((groups, rows, band), lambda i, *s: (0, 0, 0)),
            scratch_shapes=[pltpu.VMEM((folds, groups * tall, band), jnp.float32)],
        ),
        compiler_params=pltpu.CompilerParams(vmem_limit_bytes=limit),
        out_shape=jax.ShapeDtypeStruct((groups, rows, band), jnp.float32),
    )(*scalars, *arrays, *factors)


CHUNKS = 2


def choose(flag, a, b):
    height, width = a.shape
    tk = step_width(width)

    def kernel(flag_ref, a_ref, b_ref, out_ref):
        @pl.when(flag_ref[0] == 1)
        def _():
            out_ref[...] = a_ref[...]

        @pl.when(flag_ref[0] != 1)
        def _():
            out_ref[...] = b_ref[...]

    return pl.pallas_call(
        kernel,
        grid_spec=pltpu.PrefetchScalarGridSpec(
            num_scalar_prefetch=1,
            grid=(width // tk,),
            in_specs=[
                pl.BlockSpec((height, tk), lambda i, flag: (0, i * flag[0])),
                pl.BlockSpec((height, tk), lambda i, flag: (0, i * (1 - flag[0]))),
            ],
            out_specs=pl.BlockSpec((height, tk), lambda i, flag: (0, i)),
        ),
        out_shape=jax.ShapeDtypeStruct(a.shape, a.dtype),
    )(flag, a, b)


def arriving(t, planes):
    if t == 1:
        return [1]
    return sorted({t, planes - t} - {1}) if 2 * t >= planes else []


def exports(planes):
    return planes == 4


def plan(planes):
    slots = lambda *js: tuple(("slot", j) for j in js)
    if exports(planes):
        near = slots(0) + (("y", 0),) + slots(1)
        inner = (("y", 1),) + slots(2) + (("y", 2),) + slots(3)
        return (
            [("0", "e", 1), ("0", "m", 1), ("bx", "y", 0), ("1", "e", 1), ("0", "y", 0), ("1", "m", 1), ("1", "y", 0)]
            + [("b", "e", 1), ("x", "e", 1), ("x", "f", 0)]
            + [("0", "y", 1), ("0", "m", 2), ("0", "e", 2), ("0", "mul", near)]
            + [("1", "y", 1), ("1", "m", 2), ("1", "e", 2), ("bx", "m", 1), ("1", "mul", near)]
            + [("x", "m", 2), ("b", "m", 2)]
            + [("0", "sel", 2), ("0", "y", 2), ("0", "e", 3)]
            + [("1", "sel", 2), ("1", "y", 2), ("1", "e", 3), ("b", "mul", slots(0, 1))]
            + [("0", "mul", (("y", 1),) + slots(2)), ("b", "e", 2)]
            + [("0", "sel", 3), ("0", "y", 3), ("x", "mul", "own")]
            + [("1", "sel", 3), ("1", "y", 3), ("b", "e", 3)]
            + [("x", "mul", "far"), ("x", "back", 0), ("0", "mul", (("y", 2),) + slots(3) + (("y", 3),))]
            + [("1", "mul", inner + (("y", 3),)), ("b", "mul", slots(2, 3))]
        )
    chunks = [str(c) for c in range(CHUNKS)]
    last = planes - 1
    steps = [("bx", "y", 0)]
    for c in chunks:
        steps += [(c, "e", 1), (c, "y", 0)] + [(c, "m", 1)] * (last > 1)
    steps += [("b", "e", 1)] + [("b", "m", 1)] * (last > 1)
    steps += [(c, "mul", slots(0)) for c in chunks]
    sent = [0]
    for t in range(1, planes):
        new = arriving(t, planes)
        if t == last:
            for j in range(2, planes):
                steps += [("b", "e", j)] + [("b", "m", j + 1)] * (1 < j < last - 1)
        for c in chunks:
            for j in new:
                steps += [(c, "sel", j)] * (j > 1) + [(c, "y", j)]
            if t < last:
                steps += [(c, "m", t + 1)] * (t + 1 < last) + [(c, "e", t + 1)]
            if t == 1 and c == chunks[-1] and last > 2:
                steps += [("b", "m", 2)]
            if sent or new:
                steps += [(c, "mul", tuple(("y", j) for j in sent) + slots(*new))]
        if t == 1:
            steps += [("b", "mul", slots(0, 1))]
        sent = new
    for t in range(2, last):
        if arriving(t, planes):
            steps += [("b", "mul", slots(*arriving(t, planes)))]
    steps += [(c, "mul", tuple(("y", j) for j in sent)) for c in chunks[:-1]]
    if last > 1:
        steps += [("b", "mul", slots(last))]
    steps += [(c, "mul", tuple(("y", j) for j in sent)) for c in chunks[-1:]]
    return steps


def body(factor_band, normals, site_mean, site_spread, site_capacity, site_kind, site_plant):
    row_size, col_size = lax.axis_size("row"), lax.axis_size("col")
    row, col = lax.axis_index("row"), lax.axis_index("col")
    planes = row_size // 2
    z, y = row // 2, row % 2
    cols, rows = normals.shape
    band = factor_band.shape[0]
    folds = 8 // math.gcd(rows, 8)
    stride = cols // folds

    side = [(r, r ^ 1) for r in range(row_size)]

    def line(neighbour):
        return [(r, 2 * neighbour(r // 2) + r % 2) for r in range(row_size)]

    even = line(lambda p: p ^ 1)
    odd = [pair for pair in line(lambda p: ((p - 1) ^ 1) + 1) if pair[0] // 2 not in (0, planes - 1)]
    send = lambda x, pairs: lax.ppermute(x, "row", pairs)
    heading = 1 - 2 * (z % 2)
    reach = jnp.where(heading == 1, planes - 1 - z, z)

    near_end = [(j <= reach).astype(jnp.int32).reshape(1) for j in range(planes)]
    outer = (z == 0) | (z == planes - 1)

    def between(pairs, take):
        return [(a, b) for a, b in pairs if take(a // 2 in (0, planes - 1))]

    inward = between(even, lambda is_outer: is_outer)
    outward = between(even, lambda is_outer: not is_outer)

    turned = normals.T
    tiles = stride // LANE
    pairs_of = lambda share: 2 * round(tiles * share / 2)
    sizes = {"x": pairs_of(18 / 128), "b": pairs_of(22 / 128)} if exports(planes) else {"b": pairs_of(20 / 128)}
    rest = tiles - sum(sizes.values())
    sizes["1"] = 2 * (rest * 9 // 44)
    sizes["0"] = rest - sizes["1"]
    begin, at = {}, 0
    for stream in sizes:
        begin[stream], at = at * LANE, at + sizes[stream]

    begin["bx"], sizes["bx"] = 0, sizes["b"] + sizes.get("x", 0)

    def piece(stream):
        start, width = begin[stream], sizes[stream] * LANE
        return jnp.concatenate(
            [turned[:, f * stride + start : f * stride + start + width] for f in range(folds)], axis=0
        )

    own = {stream: piece(stream) for stream in ("0", "bx", "1")}
    have = {(stream, "slot", 0): own[stream] for stream in ("0", "1")}
    parts = [[[], []] for _ in range(planes)]

    def starts_of(stream):
        return [(0, f * stride + begin[stream]) for f in range(folds)]

    def cut(stream, block):
        return block[:, begin[stream] : begin[stream] + sizes[stream] * LANE]

    def multiply(stream, wanted):
        blocks, places = [], []
        for kind, j in wanted:
            if stream == "b" and j > 1:
                blocks.append((near_end[j], have["b", "e", j], have["b", "m", planes - j]))
            else:
                blocks.append(have[stream, kind, j])
            places += [(j, 0), (j, 1)] if stream == "b" else [(j, int(kind == "y"))]
        got = products(blocks, [factor_band] * folds, starts_of(stream), rows, band, sizes[stream] * LANE)
        for g, (j, q) in enumerate(places):
            parts[j][q].append(got[g])

    def multiply_exported(whose):
        blocks = [have["x", "slot", 0], have["x", "e", 1], have["bx", "m", 1], have["x", "m", 2]]
        places = [(j % planes, q) for j in (0, 1, -1, -2) for q in (0, 1)]
        slot, other = jnp.array(places, jnp.int32).T
        order = 2 * jnp.mod(z + heading * slot, planes) + (y + other) % 2
        factors, starts = [factor_band] * folds, starts_of("x")
        if whose == "far":
            factors, starts = [have["x", "f", 0]] * folds, [(f * band, 0) for f in range(folds)]
        sums = products(blocks, factors, starts, rows, band, sizes["x"] * LANE, order, whose == "far", limit=66_900_000 if whose == "far" else None)
        have["x", whose, 0] = sums

    def place(sums):
        placed = []
        for plane in range(planes):
            at = jnp.mod(heading * (plane - z), planes)
            mine, other = sums[0]
            for j in range(1, planes):
                mine = jnp.where(at == j, sums[j][0], mine)
                other = jnp.where(at == j, sums[j][1], other)
            placed += [jnp.where(y == 0, mine, other), jnp.where(y == 0, other, mine)]
        return jnp.stack(placed)

    for step in plan(planes):
        stream, move, j = step
        if move == "mul":
            multiply_exported(j) if stream == "x" else multiply(stream, j)
        elif move == "back":
            back = send(have["x", "far", 0], outward)
        elif move == "f":
            strips = [factor_band[:, left : left + sizes["x"] * LANE] for _, left in starts_of("x")]
            have[step] = send(jnp.concatenate(strips, axis=0), inward)
        elif move == "sel":
            have[stream, "slot", j] = choose(near_end[j], have[stream, "e", j], have[stream, "m", planes - j])
        elif step == ("bx", "y", 0):
            have["bx", "slot", 0] = jnp.concatenate([own["bx"], send(own["bx"], side)], axis=0)
            for part in ("b", "x"):
                if part in sizes:
                    have[part, "slot", 0] = cut(part, have["bx", "slot", 0])
        elif move == "y":
            have[step] = send(have[stream, "slot", j], side)
        else:
            came = have[stream, "m" if move == "e" else "e", j - 1] if j > 1 else have[stream, "slot", 0]
            pairs = odd if move == "m" else inward if stream == "x" else even
            if exports(planes) and move == "e" and j > 1:
                pairs = outward
            have[step] = send(came, pairs)
            if stream == "bx":
                for part in ("b", "x"):
                    have[part, move, j] = cut(part, have[step])
            if move == "e" and j == 1:
                have[stream, "slot", 1] = have[step]

    total = place([[sum(terms) for terms in pair] for pair in parts])
    if exports(planes):
        total = total + jnp.where(outer, back, have["x", "own", 0])
    share = rows * row_size // col_size
    total = total.reshape(col_size, share, band)

    samples = lax.dynamic_index_in_dim(total, col, 0, keepdims=False)
    for k in range(1, col_size):
        pairs = [(c, c ^ k) for c in range(col_size)]
        samples = samples + lax.ppermute(lax.dynamic_index_in_dim(total, col ^ k, 0, keepdims=False), "col", pairs)

    speed = site_mean[None, :] + site_spread[None, :] * samples
    positive = jnp.maximum(speed, 0.0)
    wind = jnp.clip((positive * positive * positive - 27.0) / (1728.0 - 27.0), 0.0, 1.0)
    solar = jnp.clip(speed / 12.0, 0.0, 1.0)
    power = jnp.where(site_kind[None, :] == 1, solar, wind) * site_capacity[None, :]

    power = jnp.concatenate([power, site_plant[None, :].astype(jnp.float32)], axis=0)
    pair = jnp.concatenate([power, send(power, side)], axis=1)
    table = jnp.concatenate(
        [pair] + [send(pair, line(lambda p, k=k: p ^ k)) for k in range(1, planes)], axis=1
    )
    plant = table[share].astype(jnp.int32)
    mine = PLANTS // row_size
    onehot = (plant[:, None] == row * mine + jnp.arange(mine, dtype=jnp.int32)[None, :]).astype(jnp.float32)
    return jnp.dot(table[:share], onehot, precision=lax.Precision.HIGHEST, preferred_element_type=jnp.float32)


def solution(mesh):
    in_specs = (P("row", "col"), P("col", "row"), P("row"), P("row"), P("row"), P("row"), P("row"))
    out_specs = P("col", "row")
    return jax.shard_map(body, mesh=mesh, in_specs=in_specs, out_specs=out_specs, check_vma=False)
```

```python
import math

import jax
import jax.numpy as jnp
from jax import lax
from jax.experimental import pallas as pl
from jax.experimental.pallas import tpu as pltpu
from jax.sharding import PartitionSpec as P


PLANTS = 2048
LANE = 128


def split_bf16(x):
    hi = x.astype(jnp.bfloat16)
    return hi, (x - hi.astype(jnp.float32)).astype(jnp.bfloat16)


def dot_t(a, b):
    return lax.dot_general(a, b, (((1,), (1,)), ((), ())), preferred_element_type=jnp.float32)


def step_width(width):
    tiles = width // LANE
    return LANE * max(d for d in range(1, 29) if tiles % d == 0 and (d < tiles or tiles == 1))


def products(blocks, factors, starts, rows, band, width, order=None, resident=False, limit=None):
    folds = len(factors)
    arrays, specs, flags, places = [], [], [], []
    tk = step_width(width)
    steps = width // tk
    total = 0
    for block in blocks:
        if isinstance(block, tuple):
            flag, a, b = block
            k = len(flags)
            flags.append(flag)
            places.append((len(arrays), k))
            arrays += [a, b]
            specs.append(pl.BlockSpec((a.shape[0], tk), lambda i, *s, k=k: (0, i * s[k][0])))
            specs.append(pl.BlockSpec((a.shape[0], tk), lambda i, *s, k=k: (0, i * (1 - s[k][0]))))
        else:
            a = block
            places.append((len(arrays), None))
            arrays.append(a)
            specs.append(pl.BlockSpec((a.shape[0], tk), lambda i, *s: (0, i)))
        total += a.shape[0]
    groups = total // (folds * rows)
    scalars = flags + ([] if order is None else [order])

    if resident:
        specs.append(pl.BlockSpec(memory_space=pltpu.VMEM))
        factors = factors[:1]
    for fold in range(0 if resident else folds):
        top, left = starts[fold]
        specs.append(
            pl.BlockSpec(
                (pl.Element(band), pl.Element(tk)),
                lambda i, *s, top=top, left=left: (top, pl.multiple_of(left + i * tk, LANE)),
            )
        )

    lows = [fold * rows // 8 * 8 for fold in range(folds)]
    tall = max(-(-(fold + 1) * rows // 8) * 8 - lows[fold] for fold in range(folds))
    lows = [min(low, folds * rows - tall) for low in lows]

    def kernel(*refs):
        scalar_refs, refs = refs[: len(scalars)], refs[len(scalars) :]
        out_ref, acc = refs[-2], refs[-1]
        factor_refs = refs[len(arrays) : len(arrays) + folds]
        step = pl.program_id(0)

        @pl.when(step == 0)
        def _():
            acc[...] = jnp.zeros_like(acc)

        taken = []
        for i, k in places:
            block = refs[i][...]
            if k is not None:
                block = jnp.where(scalar_refs[k][0] == 1, block, refs[i + 1][...])
            taken += [block[top : top + folds * rows] for top in range(0, block.shape[0], folds * rows)]
        for fold in range(folds):
            hi, lo = split_bf16(jnp.concatenate([t[lows[fold] : lows[fold] + tall] for t in taken], axis=0))
            if resident:
                top, left = starts[fold]
                strip = factor_refs[0][top : top + band, pl.ds(pl.multiple_of(left + step * tk, LANE), tk)]
            else:
                strip = factor_refs[fold][...]
            f_hi, f_lo = split_bf16(strip)
            first = dot_t(jnp.concatenate([hi, lo], axis=0), f_hi)
            acc[fold] += first[: groups * tall] + (first[groups * tall :] + dot_t(hi, f_lo))

        @pl.when(step == steps - 1)
        def _():
            for g in range(groups):
                base = [g * tall + fold * rows - lows[fold] for fold in range(folds)]
                out_ref[g if order is None else scalar_refs[-1][g]] = sum(
                    acc[fold, base[fold] : base[fold] + rows] for fold in range(folds)
                )

    return pl.pallas_call(
        kernel,
        grid_spec=pltpu.PrefetchScalarGridSpec(
            num_scalar_prefetch=len(scalars),
            grid=(steps,),
            in_specs=specs,
            out_specs=pl.BlockSpec((groups, rows, band), lambda i, *s: (0, 0, 0)),
            scratch_shapes=[pltpu.VMEM((folds, groups * tall, band), jnp.float32)],
        ),
        compiler_params=pltpu.CompilerParams(vmem_limit_bytes=limit),
        out_shape=jax.ShapeDtypeStruct((groups, rows, band), jnp.float32),
    )(*scalars, *arrays, *factors)


CHUNKS = 2


def choose(flag, a, b):
    height, width = a.shape
    tk = step_width(width)

    def kernel(flag_ref, a_ref, b_ref, out_ref):
        @pl.when(flag_ref[0] == 1)
        def _():
            out_ref[...] = a_ref[...]

        @pl.when(flag_ref[0] != 1)
        def _():
            out_ref[...] = b_ref[...]

    return pl.pallas_call(
        kernel,
        grid_spec=pltpu.PrefetchScalarGridSpec(
            num_scalar_prefetch=1,
            grid=(width // tk,),
            in_specs=[
                pl.BlockSpec((height, tk), lambda i, flag: (0, i * flag[0])),
                pl.BlockSpec((height, tk), lambda i, flag: (0, i * (1 - flag[0]))),
            ],
            out_specs=pl.BlockSpec((height, tk), lambda i, flag: (0, i)),
        ),
        out_shape=jax.ShapeDtypeStruct(a.shape, a.dtype),
    )(flag, a, b)


def arriving(t, planes):
    if t == 1:
        return [1]
    return sorted({t, planes - t} - {1}) if 2 * t >= planes else []


def exports(planes):
    return planes == 4


def plan(planes):
    slots = lambda *js: tuple(("slot", j) for j in js)
    if exports(planes):
        near = slots(0) + (("y", 0),) + slots(1)
        inner = (("y", 1),) + slots(2) + (("y", 2),) + slots(3)
        return (
            [("0", "e", 1), ("0", "m", 1), ("bx", "y", 0), ("1", "e", 1), ("0", "y", 0), ("1", "m", 1), ("1", "y", 0)]
            + [("b", "e", 1), ("x", "e", 1), ("x", "f", 0)]
            + [("0", "y", 1), ("0", "m", 2), ("0", "e", 2), ("0", "mul", near)]
            + [("1", "y", 1), ("1", "m", 2), ("1", "e", 2), ("bx", "m", 1), ("1", "mul", near)]
            + [("x", "m", 2), ("b", "m", 2)]
            + [("0", "sel", 2), ("0", "y", 2), ("0", "e", 3)]
            + [("1", "sel", 2), ("1", "y", 2), ("1", "e", 3), ("b", "mul", slots(0, 1))]
            + [("0", "mul", (("y", 1),) + slots(2)), ("b", "e", 2)]
            + [("0", "sel", 3), ("0", "y", 3), ("x", "mul", "own")]
            + [("1", "sel", 3), ("1", "y", 3), ("b", "e", 3)]
            + [("x", "mul", "far"), ("x", "back", 0), ("0", "mul", (("y", 2),) + slots(3) + (("y", 3),))]
            + [("1", "mul", inner + (("y", 3),)), ("b", "mul", slots(2, 3))]
        )
    chunks = [str(c) for c in range(CHUNKS)]
    last = planes - 1
    steps = [("bx", "y", 0)]
    for c in chunks:
        steps += [(c, "e", 1), (c, "y", 0)] + [(c, "m", 1)] * (last > 1)
    steps += [("b", "e", 1)] + [("b", "m", 1)] * (last > 1)
    steps += [(c, "mul", slots(0)) for c in chunks]
    sent = [0]
    for t in range(1, planes):
        new = arriving(t, planes)
        if t == last:
            for j in range(2, planes):
                steps += [("b", "e", j)] + [("b", "m", j + 1)] * (1 < j < last - 1)
        for c in chunks:
            for j in new:
                steps += [(c, "sel", j)] * (j > 1) + [(c, "y", j)]
            if t < last:
                steps += [(c, "m", t + 1)] * (t + 1 < last) + [(c, "e", t + 1)]
            if t == 1 and c == chunks[-1] and last > 2:
                steps += [("b", "m", 2)]
            if sent or new:
                steps += [(c, "mul", tuple(("y", j) for j in sent) + slots(*new))]
        if t == 1:
            steps += [("b", "mul", slots(0, 1))]
        sent = new
    for t in range(2, last):
        if arriving(t, planes):
            steps += [("b", "mul", slots(*arriving(t, planes)))]
    steps += [(c, "mul", tuple(("y", j) for j in sent)) for c in chunks[:-1]]
    if last > 1:
        steps += [("b", "mul", slots(last))]
    steps += [(c, "mul", tuple(("y", j) for j in sent)) for c in chunks[-1:]]
    return steps


def body(factor_band, normals, site_mean, site_spread, site_capacity, site_kind, site_plant):
    row_size, col_size = lax.axis_size("row"), lax.axis_size("col")
    row, col = lax.axis_index("row"), lax.axis_index("col")
    planes = row_size // 2
    z, y = row // 2, row % 2
    cols, rows = normals.shape
    band = factor_band.shape[0]
    folds = 8 // math.gcd(rows, 8)
    stride = cols // folds

    side = [(r, r ^ 1) for r in range(row_size)]

    def line(neighbour):
        return [(r, 2 * neighbour(r // 2) + r % 2) for r in range(row_size)]

    even = line(lambda p: p ^ 1)
    odd = [pair for pair in line(lambda p: ((p - 1) ^ 1) + 1) if pair[0] // 2 not in (0, planes - 1)]
    send = lambda x, pairs: lax.ppermute(x, "row", pairs)
    heading = 1 - 2 * (z % 2)
    reach = jnp.where(heading == 1, planes - 1 - z, z)

    near_end = [(j <= reach).astype(jnp.int32).reshape(1) for j in range(planes)]
    outer = (z == 0) | (z == planes - 1)

    def between(pairs, take):
        return [(a, b) for a, b in pairs if take(a // 2 in (0, planes - 1))]

    inward = between(even, lambda is_outer: is_outer)
    outward = between(even, lambda is_outer: not is_outer)

    turned = normals.T
    tiles = stride // LANE
    pairs_of = lambda share: 2 * round(tiles * share / 2)
    sizes = {"x": pairs_of(18 / 128), "b": pairs_of(22 / 128)} if exports(planes) else {"b": pairs_of(20 / 128)}
    rest = tiles - sum(sizes.values())
    sizes["1"] = 2 * (rest * 9 // 44)
    sizes["0"] = rest - sizes["1"]
    begin, at = {}, 0
    for stream in sizes:
        begin[stream], at = at * LANE, at + sizes[stream]

    begin["bx"], sizes["bx"] = 0, sizes["b"] + sizes.get("x", 0)

    def piece(stream):
        start, width = begin[stream], sizes[stream] * LANE
        return jnp.concatenate(
            [turned[:, f * stride + start : f * stride + start + width] for f in range(folds)], axis=0
        )

    own = {stream: piece(stream) for stream in ("0", "bx", "1")}
    have = {(stream, "slot", 0): own[stream] for stream in ("0", "1")}
    parts = [[[], []] for _ in range(planes)]

    def starts_of(stream):
        return [(0, f * stride + begin[stream]) for f in range(folds)]

    def cut(stream, block):
        return block[:, begin[stream] : begin[stream] + sizes[stream] * LANE]

    def multiply(stream, wanted):
        blocks, places = [], []
        for kind, j in wanted:
            if stream == "b" and j > 1:
                blocks.append((near_end[j], have["b", "e", j], have["b", "m", planes - j]))
            else:
                blocks.append(have[stream, kind, j])
            places += [(j, 0), (j, 1)] if stream == "b" else [(j, int(kind == "y"))]
        got = products(blocks, [factor_band] * folds, starts_of(stream), rows, band, sizes[stream] * LANE)
        for g, (j, q) in enumerate(places):
            parts[j][q].append(got[g])

    def multiply_exported(whose):
        blocks = [have["x", "slot", 0], have["x", "e", 1], have["bx", "m", 1], have["x", "m", 2]]
        places = [(j % planes, q) for j in (0, 1, -1, -2) for q in (0, 1)]
        slot, other = jnp.array(places, jnp.int32).T
        order = 2 * jnp.mod(z + heading * slot, planes) + (y + other) % 2
        factors, starts = [factor_band] * folds, starts_of("x")
        if whose == "far":
            factors, starts = [have["x", "f", 0]] * folds, [(f * band, 0) for f in range(folds)]
        sums = products(blocks, factors, starts, rows, band, sizes["x"] * LANE, order, whose == "far", limit=66_900_000 if whose == "far" else None)
        have["x", whose, 0] = sums

    def place(sums):
        placed = []
        for plane in range(planes):
            at = jnp.mod(heading * (plane - z), planes)
            mine, other = sums[0]
            for j in range(1, planes):
                mine = jnp.where(at == j, sums[j][0], mine)
                other = jnp.where(at == j, sums[j][1], other)
            placed += [jnp.where(y == 0, mine, other), jnp.where(y == 0, other, mine)]
        return jnp.stack(placed)

    for step in plan(planes):
        stream, move, j = step
        if move == "mul":
            multiply_exported(j) if stream == "x" else multiply(stream, j)
        elif move == "back":
            back = send(have["x", "far", 0], outward)
        elif move == "f":
            strips = [factor_band[:, left : left + sizes["x"] * LANE] for _, left in starts_of("x")]
            have[step] = send(jnp.concatenate(strips, axis=0), inward)
        elif move == "sel":
            have[stream, "slot", j] = choose(near_end[j], have[stream, "e", j], have[stream, "m", planes - j])
        elif step == ("bx", "y", 0):
            have["bx", "slot", 0] = jnp.concatenate([own["bx"], send(own["bx"], side)], axis=0)
            for part in ("b", "x"):
                if part in sizes:
                    have[part, "slot", 0] = cut(part, have["bx", "slot", 0])
        elif move == "y":
            have[step] = send(have[stream, "slot", j], side)
        else:
            came = have[stream, "m" if move == "e" else "e", j - 1] if j > 1 else have[stream, "slot", 0]
            pairs = odd if move == "m" else inward if stream == "x" else even
            if exports(planes) and move == "e" and j > 1:
                pairs = outward
            have[step] = send(came, pairs)
            if stream == "bx":
                for part in ("b", "x"):
                    have[part, move, j] = cut(part, have[step])
            if move == "e" and j == 1:
                have[stream, "slot", 1] = have[step]

    total = place([[sum(terms) for terms in pair] for pair in parts])
    if exports(planes):
        total = total + jnp.where(outer, back, have["x", "own", 0])
    share = rows * row_size // col_size
    total = total.reshape(col_size, share, band)

    samples = lax.dynamic_index_in_dim(total, col, 0, keepdims=False)
    for k in range(1, col_size):
        pairs = [(c, c ^ k) for c in range(col_size)]
        samples = samples + lax.ppermute(lax.dynamic_index_in_dim(total, col ^ k, 0, keepdims=False), "col", pairs)

    speed = site_mean[None, :] + site_spread[None, :] * samples
    positive = jnp.maximum(speed, 0.0)
    wind = jnp.clip((positive * positive * positive - 27.0) / (1728.0 - 27.0), 0.0, 1.0)
    solar = jnp.clip(speed / 12.0, 0.0, 1.0)
    power = jnp.where(site_kind[None, :] == 1, solar, wind) * site_capacity[None, :]

    power = jnp.concatenate([power, site_plant[None, :].astype(jnp.float32)], axis=0)
    pair = jnp.concatenate([power, send(power, side)], axis=1)
    came = []
    for k in range(1, planes):
        came.append(send(pair, line(lambda p, k=k: p ^ k)))
    table = jnp.concatenate([pair] + came, axis=1)
    plant = table[share].astype(jnp.int32)
    mine = PLANTS // row_size
    onehot = (plant[:, None] == row * mine + jnp.arange(mine, dtype=jnp.int32)[None, :]).astype(jnp.float32)
    return jnp.dot(table[:share], onehot, precision=lax.Precision.HIGHEST, preferred_element_type=jnp.float32)


def solution(mesh):
    in_specs = (P("row", "col"), P("col", "row"), P("row"), P("row"), P("row"), P("row"), P("row"))
    out_specs = P("col", "row")
    return jax.shard_map(body, mesh=mesh, in_specs=in_specs, out_specs=out_specs, check_vma=False)
```
